512 devices in a mesh: dom: 128 (over z, y, core), wa: 4 (over x).
Axes of the slice: x: 4, y: 8, z: 8, core: 2. Of those that a mesh axis runs over, the one named last changes fastest.
Arguments:
- bond_feats: bfloat16 [32768, 256], P('dom'), may hold values from -6 to 6
- cotangent: bfloat16 [32768, 256], P('dom', 'wa'), may hold values from -6 to 6
- bond_count: int32 [128], P('dom'), may hold values from 128 to 256, as said below
- source: int32 [393216], P('dom'), may hold values from 0 to 319, as said below
- cosine: float32 [393216], P('dom'), may hold values from -1 to 1
- w_source: bfloat16 [256, 256], P(None, 'wa'), may hold values from -0.375 to 0.375
- w_target: bfloat16 [256, 256], P(None, 'wa'), may hold values from -0.375 to 0.375
- w_message: bfloat16 [256, 256], P(None, 'wa'), may hold values from -0.375 to 0.375
- w_self: bfloat16 [256, 256], P(None, 'wa'), may hold values from -0.375 to 0.375
- gate_angle: float32 [256], P('wa'), may hold values from -4 to 4
Outputs:
- bond_grad: bfloat16 [32768, 256], P('dom', 'wa')
- grad_source: float32 [256, 256], P('dom', 'wa')
- grad_target: float32 [256, 256], P('dom', 'wa')
- grad_message: float32 [256, 256], P('dom', 'wa')
- grad_self: float32 [256, 256], P('dom', 'wa')
- grad_gate: float32 [256], P('wa')
The draws below stay inside these ranges and needn't reach their ends.
Inputs may be any that keep to these rules, and one draw needn't show every extreme that they name: `bond_count`: every domain has 128 or more live bonds; some domain has all 256 live. `source`: each angle's other bond is a live row of the extended block of its domain: a ghost row (below 32 or at 288 or above) or 32 plus a live own row.
All inputs are finite; a program needn't handle non-finite values.
Results may differ from the reference program's by a relative error of at most 0.0085.
Values may be sent and summed in bfloat16 or wider, within the bound.
No kernel may reach another device: no remote copies, remote signals or barrier semaphores. Data moves between devices by JAX's collectives and lax.ppermute only.
A program may use at most 64 MiB of HBM per device.

```python
import jax
import jax.numpy as jnp
from jax import lax

D = 256
BONDS_DOM = 256
ARITY = 12
GHOST = 32
BONDS = 32768
ANGLES = 393216


def shared_layout(key):
    domains = BONDS // BONDS_DOM
    counts = jax.random.randint(jax.random.fold_in(key, 11), (domains,), BONDS_DOM // 2, BONDS_DOM + 1)
    fullest = jax.random.randint(jax.random.fold_in(key, 12), (), 0, domains)
    counts = jnp.where(jnp.arange(domains, dtype=jnp.int32) == fullest, BONDS_DOM, counts).astype(jnp.int32)
    per_angle = jnp.broadcast_to(counts[:, None], (domains, ARITY * BONDS_DOM)).reshape(ANGLES)
    ghost_flag = jax.random.randint(jax.random.fold_in(key, 13), (ANGLES,), 0, 4) == 0
    ghost_pick = jax.random.randint(jax.random.fold_in(key, 14), (ANGLES,), 0, 2 * GHOST)
    ghost_index = jnp.where(ghost_pick < GHOST, ghost_pick, BONDS_DOM + ghost_pick)
    uniform_pick = jax.random.randint(jax.random.fold_in(key, 15), (ANGLES,), 0, per_angle)
    own_row = jnp.where(uniform_pick < per_angle - GHOST, uniform_pick, uniform_pick - (per_angle - GHOST) + BONDS_DOM - GHOST)
    sources = jnp.where(ghost_flag, ghost_index, GHOST + own_row).astype(jnp.int32)
    return (counts, sources)


def draw_bond_count(key, part):
    return shared_layout(key)[0]


def draw_source(key, part):
    return shared_layout(key)[1]


def level_of(own_key, dims, pieces, smallest, largest):
    level = 1.0
    for axis_at, shards_of in pieces:
        heights = jax.random.uniform(jax.random.fold_in(jax.random.fold_in(own_key, 6), axis_at), (shards_of,), jnp.float32, smallest / len(pieces), largest / len(pieces))
        level = level * jnp.repeat(jnp.exp(heights), dims[axis_at] // shards_of).reshape((-1,) + (1,) * (len(dims) - 1 - axis_at))
    return level


def normal_values(key, extent, scale, limit, shards=(), held_as=jnp.bfloat16):
    values = jax.random.normal(key, extent, jnp.float32) * scale
    if len(shards) > 0:
        values = level_of(key, extent, shards, -0.22, 0.18) * values
    return jnp.clip(values, min=-limit, max=limit).astype(held_as)


def setup_inputs(seed: int = 0) -> dict:
    key_list = jax.random.split(jax.random.key(seed), 11)
    return {
        "bond_feats": normal_values(key_list[0], (BONDS, D), 1.0, 6.0, ((0, 128),)),
        "cotangent": normal_values(key_list[1], (BONDS, D), 1.0, 6.0, ((0, 128), (1, 4))),
        "bond_count": draw_bond_count(jax.random.fold_in(key_list[10], 71), 0),
        "source": draw_source(jax.random.fold_in(key_list[10], 71), 0),
        "cosine": jnp.clip(jax.random.uniform(key_list[4], (ANGLES,), jnp.float32, -1.0, 1.0) * level_of(key_list[4], (ANGLES,), ((0, 128),), -0.4, 0.0), -1.0, 1.0),
        "w_source": normal_values(key_list[5], (D, D), D ** -0.5, 0.375, ((1, 4),)),
        "w_target": normal_values(key_list[6], (D, D), D ** -0.5, 0.375, ((1, 4),)),
        "w_message": normal_values(key_list[7], (D, D), D ** -0.5, 0.375, ((1, 4),)),
        "w_self": normal_values(key_list[8], (D, D), D ** -0.5, 0.375, ((1, 4),)),
        "gate_angle": normal_values(key_list[9], (D,), 1.0, 4.0, ((0, 4),), jnp.float32),
    }


epsilon = 1e-6


def silu_slope(values):
    sigma = jax.nn.sigmoid(values)
    return sigma * (1.0 + values * (1.0 - sigma))


def reference(bond_feats, cotangent, bond_count, source, cosine, w_source, w_target, w_message, w_self, gate_angle):
    domains = BONDS // BONDS_DOM
    width = bond_feats.shape[1]
    blocks = bond_feats.reshape(domains, BONDS_DOM, width)
    before = jnp.roll(blocks, 1, axis=0)[:, BONDS_DOM - GHOST:]
    after = jnp.roll(blocks, -1, axis=0)[:, :GHOST]
    extended_all = jnp.concatenate([before, blocks, after], axis=1)
    cot_blocks = cotangent.reshape(domains, BONDS_DOM, width)
    source_blocks = source.reshape(domains, ARITY * BONDS_DOM)
    cosine_blocks = cosine.reshape(domains, ARITY * BONDS_DOM)
    ext_rows = BONDS_DOM + 2 * GHOST

    def spread(values):
        return jnp.broadcast_to(values[:, None, :], (BONDS_DOM, ARITY, values.shape[1])).reshape(ARITY * BONDS_DOM, values.shape[1])

    def per_bond(values):
        return values.reshape(BONDS_DOM, ARITY, values.shape[1]).sum(axis=1)

    def domain_step(carry, inputs):
        extended, own_rows, cot_rows, count, sources, cosines = inputs
        rows = jnp.arange(BONDS_DOM, dtype=jnp.int32)
        live = ((rows < count - GHOST) | (rows >= BONDS_DOM - GHOST)).astype(jnp.float32)
        alive = jnp.broadcast_to(live[:, None], (BONDS_DOM, ARITY)).reshape(ARITY * BONDS_DOM)[:, None]
        proj_source = jnp.dot(extended, w_source, preferred_element_type=jnp.float32)
        proj_message = jnp.dot(extended, w_message, preferred_element_type=jnp.float32)
        proj_target = jnp.dot(own_rows, w_target, preferred_element_type=jnp.float32)
        base = jnp.dot(own_rows, w_self, preferred_element_type=jnp.float32)
        picked_source = jnp.take(proj_source, sources, axis=0)
        picked_message = jnp.take(proj_message, sources, axis=0)
        pre = picked_source + spread(proj_target) + cosines[:, None] * gate_angle[None, :]
        sigma = jax.nn.sigmoid(pre)
        gated = sigma * alive
        numer = per_bond(gated * picked_message)
        denom = per_bond(gated) + epsilon
        aggregate = numer / denom
        hidden = base + aggregate
        cot_live = cot_rows.astype(jnp.float32) * live[:, None]
        dhidden = cot_live * silu_slope(hidden)
        dnumer = dhidden / denom
        ddenom = -dhidden * aggregate / denom
        dgate = spread(dnumer) * picked_message + spread(ddenom)
        dmessage = gated * spread(dnumer)
        dpre = dgate * sigma * (1.0 - sigma) * alive
        dsource = jax.ops.segment_sum(dpre, sources, num_segments=ext_rows)
        dmsg_rows = jax.ops.segment_sum(dmessage, sources, num_segments=ext_rows)
        dtarget = per_bond(dpre)
        gate_term = jnp.sum(cosines[:, None] * dpre, axis=0)
        round_source = dsource.astype(jnp.bfloat16)
        round_message = dmsg_rows.astype(jnp.bfloat16)
        round_target = dtarget.astype(jnp.bfloat16)
        round_hidden = dhidden.astype(jnp.bfloat16)
        grad_one = jnp.dot(extended.T, round_source, preferred_element_type=jnp.float32)
        grad_two = jnp.dot(own_rows.T, round_target, preferred_element_type=jnp.float32)
        grad_four = jnp.dot(extended.T, round_message, preferred_element_type=jnp.float32)
        grad_five = jnp.dot(own_rows.T, round_hidden, preferred_element_type=jnp.float32)
        dext = jnp.dot(round_source, w_source.T, preferred_element_type=jnp.float32) + jnp.dot(round_message, w_message.T, preferred_element_type=jnp.float32)
        down = jnp.dot(round_target, w_target.T, preferred_element_type=jnp.float32) + jnp.dot(round_hidden, w_self.T, preferred_element_type=jnp.float32)
        new_carry = (carry[0] + grad_one, carry[1] + grad_two, carry[2] + grad_four, carry[3] + grad_five, carry[4] + gate_term)
        return new_carry, (dext, down + cot_live)

    zeros_square = jnp.zeros((width, width), jnp.float32)
    start = (zeros_square, zeros_square, zeros_square, zeros_square, jnp.zeros((width,), jnp.float32))
    totals, outputs = lax.scan(domain_step, start, (extended_all, blocks, cot_blocks, bond_count, source_blocks, cosine_blocks))
    dext_all, own_all = outputs
    own_total = own_all + dext_all[:, GHOST:GHOST + BONDS_DOM]
    from_next = jnp.roll(dext_all[:, :GHOST], -1, axis=0)
    from_prev = jnp.roll(dext_all[:, GHOST + BONDS_DOM:], 1, axis=0)
    own_total = own_total.at[:, BONDS_DOM - GHOST:].add(from_next)
    own_total = own_total.at[:, :GHOST].add(from_prev)
    bond_grad = own_total.reshape(BONDS, width).astype(jnp.bfloat16)
    return bond_grad, totals[0], totals[1], totals[2], totals[3], totals[4]
```

```python
import jax
import jax.numpy as jnp
from jax import lax
from jax.experimental import pallas as pl
from jax.experimental.pallas import tpu as pltpu
from jax.sharding import Mesh
from jax.sharding import PartitionSpec as P

ARITY = 12
GHOST = 32
CAP = 256
EXT = CAP + 2 * GHOST
DOM = ("dom_0", "dom_1", "dom_2")
NDOM = 128
EPS = 1e-06
F32 = jnp.float32
BF16 = jnp.bfloat16


def dot(a, b, ca=1, cb=0):
    return lax.dot_general(a, b, (((ca,), (cb,)), ((), ())), preferred_element_type=F32)


def sigmoid(v):
    return 1.0 / (1.0 + jnp.exp(-v))


def angle_kernel(
    meta,
    h_ref,
    ga_ref,
    gb_ref,
    cot_ref,
    src_ref,
    cos_ref,
    ws_ref,
    wm_ref,
    wt_ref,
    wf_ref,
    gate_w_ref,
    whole_ref,
    grads_ref,
    gate_ref,
    hot_ref,
    sig_ref,
    msg_ref,
):
    count = meta[0]
    odd = meta[1]
    h = h_ref[...]
    gh = jnp.concatenate([ga_ref[...], gb_ref[...]], axis=0)
    h_t = h.T
    gh_t = gh.T
    w_t = jnp.concatenate([ws_ref[...], wm_ref[...], wt_ref[...], wf_ref[...]], axis=0)
    own = dot(w_t, h_t)
    far = dot(w_t[:128], gh_t)
    own_hi = own[:128].astype(BF16)
    own_lo = (own[:128] - own_hi.astype(F32)).astype(BF16)
    far_hi = far.astype(BF16)
    far_lo = (far - far_hi.astype(F32)).astype(BF16)
    table_own = jnp.concatenate([own_hi, own_lo], axis=0)
    table_far = jnp.concatenate([far_hi, far_lo], axis=0)
    q2 = own[128:192]
    base = own[192:256]

    bond = lax.broadcasted_iota(jnp.int32, (1, CAP), 1)
    live = ((bond < count - GHOST) | (bond >= CAP - GHOST)).astype(F32)
    src = src_ref[...]
    low_base = jnp.where(odd == 1, CAP, CAP + GHOST)
    high_base = jnp.where(odd == 1, CAP + GHOST, CAP)
    row = jnp.where(
        src < GHOST,
        src + low_base,
        jnp.where(src >= CAP + GHOST, src - (CAP + GHOST) + high_base, src - GHOST),
    )
    row_id = lax.broadcasted_iota(jnp.int32, (EXT, CAP), 0)
    gate_w = gate_w_ref[...]

    num = jnp.zeros((64, CAP), F32)
    den = jnp.zeros((64, CAP), F32)
    for k in range(ARITY):
        hot = (row_id == row[k : k + 1]).astype(F32).astype(BF16)
        hot_ref[k] = hot
        picked = dot(table_own, hot[:CAP]) + dot(table_far, hot[CAP:])
        p1 = picked[0:64] + picked[128:192]
        p4 = picked[64:128] + picked[192:256]
        sig = sigmoid(p1 + q2 + gate_w * cos_ref[k : k + 1])
        gate = sig * live
        num += gate * p4
        den += gate
        sig_ref[k] = sig
        msg_ref[k] = p4
    den = den + EPS
    agg = num / den
    z = base + agg
    s = sigmoid(z)
    dz = cot_ref[...].astype(F32) * live * (s * (1.0 + z * (1.0 - s)))
    dnum = dz / den
    dden = -(dnum * agg)

    dq2 = jnp.zeros((64, CAP), F32)
    dgw = jnp.zeros((64, CAP), F32)
    acc = jnp.zeros((EXT, 128), F32)
    for k in range(ARITY):
        sig = sig_ref[k]
        gate = sig * live
        dgate = dnum * msg_ref[k] + dden
        dmsg = gate * dnum
        dpre = dgate * gate * (1.0 - sig)
        dq2 += dpre
        dgw += dpre * cos_ref[k : k + 1]
        both = jnp.concatenate([dpre, dmsg], axis=0).astype(BF16)
        acc += dot(hot_ref[k], both, 1, 1)
    edge = acc.astype(BF16)
    bonds = jnp.concatenate([dq2, dz], axis=0).astype(BF16).T
    full = jnp.concatenate([edge[:CAP], bonds], axis=1)
    edge_far = edge[CAP:]
    whole_ref[:, :CAP] = dot(full, w_t).astype(BF16).T
    whole_ref[:, CAP:] = dot(edge_far, w_t[:128]).astype(BF16).T
    grads = dot(h_t, full)
    extra = dot(gh_t, edge_far)
    grads_ref[:, :128] = (grads[:, :128] + extra).astype(BF16)
    grads_ref[:, 128:] = grads[:, 128:].astype(BF16)
    gate_ref[...] = jnp.sum(dgw, axis=1, keepdims=True)


def angle_stage(meta, h, ga, gb, cot_t, src, cos, ws, wm, wt, wf, gate_w):
    vmem = pl.BlockSpec(memory_space=pltpu.VMEM)
    return pl.pallas_call(
        angle_kernel,
        out_shape=(
            jax.ShapeDtypeStruct((256, EXT), BF16),
            jax.ShapeDtypeStruct((256, 256), BF16),
            jax.ShapeDtypeStruct((64, 1), F32),
        ),
        in_specs=[pl.BlockSpec(memory_space=pltpu.SMEM)] + [vmem] * 11,
        out_specs=(vmem, vmem, vmem),
        scratch_shapes=[
            pltpu.VMEM((ARITY, EXT, CAP), BF16),
            pltpu.VMEM((ARITY, 64, CAP), F32),
            pltpu.VMEM((ARITY, 64, CAP), F32),
        ],
        name="angle_stage",
    )(meta, h, ga, gb, cot_t, src, cos, ws, wm, wt, wf, gate_w)


def swap_core(x):
    return lax.ppermute(x, DOM, [(i, i ^ 1) for i in range(NDOM)])


def swap_chip(x):
    return lax.ppermute(x, DOM, [(i, (i + 1) % NDOM if i % 2 else (i - 1) % NDOM) for i in range(NDOM)])


def per_device(
    bond_feats,
    cotangent,
    bond_count,
    source,
    cosine,
    w_source,
    w_target,
    w_message,
    w_self,
    gate_angle,
):
    odd = lax.axis_index("dom_2")
    first, last = bond_feats[:GHOST], bond_feats[CAP - GHOST :]
    is_odd = odd == 1
    ghost_a = swap_core(jnp.where(is_odd, first, last))
    ghost_b = swap_chip(jnp.where(is_odd, last, first))
    meta = jnp.stack([bond_count[0], odd.astype(jnp.int32)])
    src = source.reshape(CAP, ARITY).T
    cos = cosine.reshape(CAP, ARITY).T
    cot_t = cotangent.T
    whole, grads, gate_term = angle_stage(
        meta,
        bond_feats,
        ghost_a,
        ghost_b,
        cot_t,
        src,
        cos,
        w_source.T,
        w_message.T,
        w_target.T,
        w_self.T,
        gate_angle[:, None],
    )
    tiles = lax.all_to_all(whole.reshape(4, 64, EXT), "wa", 0, 0, tiled=True)
    summed = tiles.astype(F32).sum(axis=0)
    back_a = swap_core(summed[:, CAP : CAP + GHOST])
    back_b = swap_chip(summed[:, CAP + GHOST :])
    gate_row = gate_term[:, 0]
    gate_hi = gate_row.astype(BF16)
    gate_lo = (gate_row - gate_hi.astype(F32)).astype(BF16)
    gate_slot = jnp.concatenate([gate_hi, gate_lo, jnp.zeros((128,), BF16)])
    slots = jnp.concatenate(
        [grads.reshape(NDOM, 256 // NDOM, 256), jnp.broadcast_to(gate_slot[None, None], (NDOM, 1, 256))], axis=1
    )
    arrived = lax.all_to_all(slots, DOM, 0, 0, tiled=True).astype(F32).sum(axis=0)
    grad_gate = arrived[-1, :64] + arrived[-1, 64:128]

    bond = jnp.arange(CAP, dtype=jnp.int32)
    count = bond_count[0]
    live = ((bond < count - GHOST) | (bond >= CAP - GHOST)).astype(F32)
    total = summed[:, :CAP] + cot_t.astype(F32) * live[None, :]
    to_first = jnp.where(is_odd, back_a, back_b)
    to_last = jnp.where(is_odd, back_b, back_a)
    added = jnp.concatenate([to_first, jnp.zeros((64, CAP - 2 * GHOST), F32), to_last], axis=1)
    bond_grad = (total + added).astype(BF16).T
    return (
        bond_grad,
        arrived[:-1, 0:64],
        arrived[:-1, 128:192],
        arrived[:-1, 64:128],
        arrived[:-1, 192:256],
        grad_gate,
    )


def solution(mesh):
    finer = Mesh(mesh.devices.reshape(8, 8, 2, mesh.shape["wa"]), ("dom_0", "dom_1", "dom_2", "wa"))
    return jax.shard_map(
        per_device,
        mesh=finer,
        in_specs=(
            P(DOM, None),
            P(DOM, "wa"),
            P(DOM),
            P(DOM),
            P(DOM),
            P(None, "wa"),
            P(None, "wa"),
            P(None, "wa"),
            P(None, "wa"),
            P("wa"),
        ),
        out_specs=(P(DOM, "wa"), P(DOM, "wa"), P(DOM, "wa"), P(DOM, "wa"), P(DOM, "wa"), P("wa")),
        check_vma=False,
    )
```

```python
import jax
import jax.numpy as jnp
from jax import lax
from jax.experimental import pallas as pl
from jax.experimental.pallas import tpu as pltpu
from jax.sharding import Mesh
from jax.sharding import PartitionSpec as P


ARITY = 12
GHOST = 32
CAP = 256
EXT = CAP + 2 * GHOST
DOM = ("dom_0", "dom_1", "dom_2")
CHIP = ("dom_0", "dom_1")
NDOM = 128
EPS = 1e-06
F32 = jnp.float32
BF16 = jnp.bfloat16
VMEM = pl.BlockSpec(memory_space=pltpu.VMEM)
SMEM = pl.BlockSpec(memory_space=pltpu.SMEM)
HBM = pl.BlockSpec(memory_space=pltpu.HBM)


def dot(a, b, ca=1, cb=0):
    return lax.dot_general(a, b, (((ca,), (cb,)), ((), ())), preferred_element_type=F32)


def sigmoid(v):
    return 1.0 / (1.0 + jnp.exp(-v))


def two_parts(v):
    high = v.astype(BF16)
    return high, (v - high.astype(F32)).astype(BF16)


def in_vmem(x):
    return pltpu.with_memory_space_constraint(x, pltpu.VMEM)


def in_hbm(x):
    return pltpu.with_memory_space_constraint(x, pltpu.HBM)


def stay(shape, dtype):
    return pltpu.VMEM(shape, dtype)


def live_row(count):
    bond = lax.broadcasted_iota(jnp.int32, (1, CAP), 1)
    return ((bond < count - GHOST) | (bond >= CAP - GHOST)).astype(F32)


def prep_kernel(
    odd_ref, count_ref, src_ref, cos_ref, h_hbm, ws_hbm, wm_hbm, wt_hbm, wf_hbm, gate_w_hbm, cot_hbm,
    hp_ref, w_ref, perm_ref, own_ref, hot_ref, part_ref, cot_live_ref,
    h_ref, gate_w_ref, cot_ref, sems,
):
    copies = [
        pltpu.make_async_copy(ref, w_ref.at[pl.ds(64 * n, 64)], sems.at[n])
        for n, ref in enumerate((ws_hbm, wm_hbm, wt_hbm, wf_hbm))
    ]
    copies.append(pltpu.make_async_copy(h_hbm, h_ref, sems.at[4]))
    copies.append(pltpu.make_async_copy(gate_w_hbm, gate_w_ref, sems.at[5]))
    copies.append(pltpu.make_async_copy(cot_hbm, cot_ref, sems.at[6]))
    for copy in copies:
        copy.start()
    odd = odd_ref[0]
    rows = 256 // NDOM
    m = lax.broadcasted_iota(jnp.int32, (256, 256), 0)
    i = lax.broadcasted_iota(jnp.int32, (256, 256), 1)
    half = jnp.where(m < 128, 1 - odd, odd)
    m = m & 127
    want = (m // rows) * (2 * rows) + rows * half + m % rows
    perm = (i == want).astype(F32).astype(BF16)
    perm_ref[...] = perm
    src = src_ref[...].T
    cos = cos_ref[...].T
    low_base = jnp.where(odd == 1, CAP, CAP + GHOST)
    high_base = jnp.where(odd == 1, CAP + GHOST, CAP)
    row = jnp.where(
        src < GHOST,
        src + low_base,
        jnp.where(src >= CAP + GHOST, src - (CAP + GHOST) + high_base, src - GHOST),
    )
    row_id = lax.broadcasted_iota(jnp.int32, (EXT, CAP), 0)
    for k in range(ARITY):
        hot_ref[k] = (row_id == row[k : k + 1]).astype(F32).astype(BF16)
    for copy in copies:
        copy.wait()
    cot_live_ref[...] = cot_ref[...].astype(F32) * live_row(count_ref[0])
    h_t = h_ref[...].T
    w_t = w_ref[...]
    hp_ref[...] = dot(perm, h_t).astype(BF16)
    own = dot(w_t, h_t)
    own_ref[...] = own[128:]
    high, low = two_parts(own[:128])
    table = jnp.concatenate([high, low], axis=0)
    eye = lax.broadcasted_iota(jnp.int32, (64, 64), 0) == lax.broadcasted_iota(jnp.int32, (64, 64), 1)
    gate_w = jnp.sum(jnp.where(eye, gate_w_ref[...], 0.0), axis=1, keepdims=True)
    for k in range(ARITY):
        picked = dot(table, hot_ref[k, :CAP])
        part_ref[k, 0:64] = picked[0:64] + picked[128:192] + (own[128:192] + gate_w * cos[k : k + 1])
        part_ref[k, 64:128] = picked[64:128] + picked[192:256]


def prep_stage(odd, count, src, cos, *held):
    return pl.pallas_call(
        prep_kernel,
        out_shape=(
            stay((256, CAP), BF16),
            stay((256, 256), BF16),
            stay((256, 256), BF16),
            stay((128, CAP), F32),
            stay((ARITY, EXT, CAP), BF16),
            stay((ARITY, 128, CAP), F32),
            stay((64, CAP), F32),
        ),
        in_specs=[SMEM, SMEM, VMEM, VMEM] + [HBM] * 7,
        out_specs=(VMEM,) * 7,
        scratch_shapes=[
            pltpu.VMEM((CAP, 256), BF16),
            pltpu.VMEM((1, 64), F32),
            pltpu.VMEM((64, CAP), BF16),
            pltpu.SemaphoreType.DMA((7,)),
        ],
        compiler_params=pltpu.CompilerParams(vmem_limit_bytes=24 << 20),
        name="prep_stage",
    )(odd, count, src, cos, *(in_hbm(x) for x in held))


def angle_kernel(
    count_ref, ga_ref, gb_ref, cos_ref, hp_ref, w_ref, perm_ref, own_ref, hot_ref, part_ref, cot_live_ref,
    whole_ref, send_ref, keep_ref,
    sig_ref, msg_ref,
):
    w_t = w_ref[...]
    gh_t = jnp.concatenate([ga_ref[...], gb_ref[...]], axis=0).T
    high, low = two_parts(dot(w_t[:128], gh_t))
    table = jnp.concatenate([high, low], axis=1)
    gh_p = dot(perm_ref[...], gh_t).astype(BF16)
    cos = cos_ref[...].T

    live = live_row(count_ref[0])
    num = jnp.zeros((64, CAP), F32)
    den = jnp.zeros((64, CAP), F32)
    for k in range(ARITY):
        far = hot_ref[k, CAP:]
        picked = dot(table, jnp.concatenate([far, far], axis=0)) + part_ref[k]
        p4 = picked[64:128]
        sig = sigmoid(picked[0:64])
        gate = sig * live
        num += gate * p4
        den += gate
        sig_ref[k] = sig
        msg_ref[k] = p4
    den = den + EPS
    agg = num / den
    z = own_ref[64:128] + agg
    s = sigmoid(z)
    dz = cot_live_ref[...] * (s * (1.0 + z * (1.0 - s)))
    dnum = dz / den
    dden = -(dnum * agg)

    dq2 = jnp.zeros((64, CAP), F32)
    dgw = jnp.zeros((64, CAP), F32)
    acc = jnp.zeros((EXT, 128), F32)
    for k in range(ARITY):
        sig = sig_ref[k]
        gate = sig * live
        dgate = dnum * msg_ref[k] + dden
        dmsg = gate * dnum
        dpre = dgate * gate * (1.0 - sig)
        dq2 += dpre
        dgw += dpre * cos[k : k + 1]
        both = jnp.concatenate([dpre, dmsg], axis=0).astype(BF16)
        acc += dot(hot_ref[k], both, 1, 1)
    edge = acc.astype(BF16)
    bonds = jnp.concatenate([dq2, dz], axis=0).astype(BF16).T
    full = jnp.concatenate([edge[:CAP], bonds], axis=1)
    edge_far = edge[CAP:]
    whole_ref[:, :CAP] = dot(full, w_t).astype(BF16).T
    whole_ref[:, CAP:] = dot(edge_far, w_t[:128]).astype(BF16).T
    grads = dot(hp_ref[...], full)
    grads = jnp.concatenate([grads[:, :128] + dot(gh_p, edge_far), grads[:, 128:]], axis=1)
    ones = jnp.ones((8, CAP), BF16)
    dgw_high, dgw_low = two_parts(dgw)
    gate = dot(ones, dgw_high, 1, 1) + dot(ones, dgw_low, 1, 1)
    keep_ref[0:128] = grads[128:256]
    keep_ref[128:136] = jnp.concatenate([gate, jnp.zeros((8, 192), F32)], axis=1)
    send_ref[0:128] = grads[0:128].astype(BF16)
    gate_high, gate_low = two_parts(gate)
    row = jnp.concatenate([gate_high, gate_low, jnp.zeros((8, 128), BF16)], axis=1)
    send_ref[128:144] = jnp.concatenate([row, row], axis=0)


def angle_stage(count, ga, gb, cos, prepared):
    return pl.pallas_call(
        angle_kernel,
        out_shape=(
            jax.ShapeDtypeStruct((256, EXT), BF16),
            jax.ShapeDtypeStruct((144, 256), BF16),
            stay((136, 256), F32),
        ),
        in_specs=[SMEM] + [VMEM] * 10,
        out_specs=(VMEM, VMEM, VMEM),
        scratch_shapes=[
            pltpu.VMEM((ARITY, 64, CAP), F32),
            pltpu.VMEM((ARITY, 64, CAP), F32),
        ],
        compiler_params=pltpu.CompilerParams(vmem_limit_bytes=24 << 20),
        name="angle_stage",
    )(count, in_vmem(ga), in_vmem(gb), cos, *prepared)


def pair_kernel(keep_ref, recv_ref, out_ref):
    out_ref[:, :256] = (keep_ref[0:128] + recv_ref[0:128].astype(F32)).astype(BF16)
    row = recv_ref[128:144].astype(F32)[0:8]
    gate = keep_ref[128:136][:, 0:64] + row[:, 0:64] + row[:, 64:128]
    high, low = two_parts(gate)
    out_ref[:, 256:] = jnp.broadcast_to(jnp.concatenate([high, low], axis=1)[0:1], (128, 128))


def pair_stage(keep, recv):
    return pl.pallas_call(
        pair_kernel,
        out_shape=jax.ShapeDtypeStruct((128, 384), BF16),
        in_specs=[VMEM, VMEM],
        out_specs=VMEM,
        compiler_params=pltpu.CompilerParams(vmem_limit_bytes=24 << 20),
        name="pair_stage",
    )(keep, in_vmem(recv))


def last_kernel(slots_ref, source_ref, target_ref, message_ref, self_ref, gate_ref):
    total = jnp.sum(slots_ref[...].astype(F32), axis=0)
    source_ref[...] = total[:, 0:64]
    message_ref[...] = total[:, 64:128]
    target_ref[...] = total[:, 128:192]
    self_ref[...] = total[:, 192:256]
    gate_ref[...] = total[0:1, 256:320] + total[0:1, 320:384]


def last_stage(slots):
    rows = slots.shape[1]
    square = jax.ShapeDtypeStruct((rows, 64), F32)
    return pl.pallas_call(
        last_kernel,
        out_shape=(square, square, square, square, jax.ShapeDtypeStruct((1, 64), F32)),
        in_specs=[VMEM],
        out_specs=(VMEM,) * 5,
        compiler_params=pltpu.CompilerParams(vmem_limit_bytes=24 << 20),
        name="last_stage",
    )(in_vmem(slots))


def swap_core(x):
    return lax.ppermute(x, DOM, [(i, i ^ 1) for i in range(NDOM)])


def swap_chip(x):
    return lax.ppermute(x, DOM, [(i, (i + 1) % NDOM if i % 2 else (i - 1) % NDOM) for i in range(NDOM)])


def per_device(
    bond_feats,
    cotangent,
    bond_count,
    source,
    cosine,
    w_source,
    w_target,
    w_message,
    w_self,
    gate_angle,
):
    odd = lax.axis_index("dom_2").astype(jnp.int32)
    is_odd = odd == 1
    first, last = bond_feats[:GHOST], bond_feats[CAP - GHOST :]
    ghost_b = swap_chip(jnp.where(is_odd, last, first))
    ghost_a = swap_core(jnp.where(is_odd, first, last))
    src = source.reshape(CAP, ARITY)
    cos = cosine.reshape(CAP, ARITY)
    prepared = prep_stage(
        odd.reshape(1),
        bond_count,
        src,
        cos,
        bond_feats,
        w_source.T,
        w_message.T,
        w_target.T,
        w_self.T,
        gate_angle[None, :],
        cotangent.T,
    )
    whole, send, keep = angle_stage(bond_count, ghost_a, ghost_b, cos, prepared)
    tiles = lax.all_to_all(whole.reshape(4, 64, EXT), "wa", 0, 0, tiled=True)
    recv = swap_core(send)
    slots = pair_stage(keep, recv).reshape(NDOM // 2, 256 // NDOM, 384)
    slots = lax.all_to_all(slots, CHIP, 0, 0, tiled=True)
    summed = tiles.astype(F32).sum(axis=0)
    back_b = swap_chip(summed[:, CAP + GHOST :])
    back_a = swap_core(summed[:, CAP : CAP + GHOST])
    g_source, g_target, g_message, g_self, g_gate = last_stage(slots)

    total = summed[:, :CAP] + prepared[-1]
    to_first = jnp.where(is_odd, back_a, back_b)
    to_last = jnp.where(is_odd, back_b, back_a)
    added = jnp.concatenate([to_first, jnp.zeros((64, CAP - 2 * GHOST), F32), to_last], axis=1)
    bond_grad = (total + added).astype(BF16).T
    return (bond_grad, g_source, g_target, g_message, g_self, g_gate[0])


def solution(mesh):
    finer = Mesh(mesh.devices.reshape(8, 8, 2, mesh.shape["wa"]), ("dom_0", "dom_1", "dom_2", "wa"))
    return jax.shard_map(
        per_device,
        mesh=finer,
        in_specs=(
            P(DOM, None),
            P(DOM, "wa"),
            P(DOM),
            P(DOM),
            P(DOM),
            P(None, "wa"),
            P(None, "wa"),
            P(None, "wa"),
            P(None, "wa"),
            P("wa"),
        ),
        out_specs=(P(DOM, "wa"), P(DOM, "wa"), P(DOM, "wa"), P(DOM, "wa"), P(DOM, "wa"), P("wa")),
        check_vma=False,
    )
```

```python
import jax
import jax.numpy as jnp
from jax import lax
from jax.experimental import pallas as pl
from jax.experimental.pallas import tpu as pltpu
from jax.sharding import Mesh
from jax.sharding import PartitionSpec as P


ARITY = 12
CHUNK = 3
GHOST = 32
CAP = 256
EXT = CAP + 2 * GHOST
DOM = ("dom_0", "dom_1", "dom_2")
CHIP = ("dom_0", "dom_1")
NDOM = 128
EPS = 1e-06
F32 = jnp.float32
BF16 = jnp.bfloat16
VMEM = pl.BlockSpec(memory_space=pltpu.VMEM)
SMEM = pl.BlockSpec(memory_space=pltpu.SMEM)
HBM = pl.BlockSpec(memory_space=pltpu.HBM)


def dot(a, b, ca=1, cb=0):
    return lax.dot_general(a, b, (((ca,), (cb,)), ((), ())), preferred_element_type=F32)


def sigmoid(v):
    return 1.0 / (1.0 + jnp.exp(-v))


def two_parts(v):
    high = v.astype(BF16)
    return high, (v - high.astype(F32)).astype(BF16)


def in_vmem(x):
    return pltpu.with_memory_space_constraint(x, pltpu.VMEM)


def in_hbm(x):
    return pltpu.with_memory_space_constraint(x, pltpu.HBM)


def stay(shape, dtype):
    return pltpu.VMEM(shape, dtype)


def live_row(count):
    bond = lax.broadcasted_iota(jnp.int32, (1, CAP), 1)
    return ((bond < count - GHOST) | (bond >= CAP - GHOST)).astype(F32)


def by_slot(src_ref, cos_ref):
    def grouped(ref):
        return jnp.concatenate([ref[pl.ds(t, 8, stride=3), :] for t in range(3)], axis=1)

    cos = grouped(cos_ref)
    one = cos.astype(BF16)
    rest = cos - one.astype(F32)
    two = rest.astype(BF16)
    three = (rest - two.astype(F32)).astype(BF16)
    middle = EXT // 2
    src = (grouped(src_ref) - middle).astype(F32)
    parts = jnp.concatenate([src, one.astype(F32), two.astype(F32), three.astype(F32)], axis=0).astype(BF16)
    spot = lax.broadcasted_iota(jnp.int32, (384, CAP), 0)
    start = (lax.broadcasted_iota(jnp.int32, (1, CAP), 1) & 31) * ARITY
    inside = (spot >= start) & (spot < start + ARITY)
    slot = lax.broadcasted_iota(jnp.int32, (16, 384), 1) % ARITY
    slot = (slot == lax.broadcasted_iota(jnp.int32, (16, 384), 0)).astype(F32).astype(BF16)
    group = lax.broadcasted_iota(jnp.int32, (32, CAP), 0)
    wanted = lax.broadcasted_iota(jnp.int32, (32, CAP), 1) >> 5
    rows = []
    for n in range(4):
        pick = (group == wanted + 8 * n).astype(F32).astype(BF16)
        spread = jnp.where(inside, dot(parts, pick, 0, 0), 0.0).astype(BF16)
        rows.append(dot(slot, spread))
    return rows[0].astype(jnp.int32) + middle, rows[1] + rows[2] + rows[3]


def prep_kernel(
    odd_ref, count_hbm, src_hbm, cos_hbm, h_hbm, ws_hbm, wm_hbm, wt_hbm, wf_hbm, gate_w_hbm, cot_hbm,
    hp_ref, w_ref, perm_ref, own_ref, hot_ref, part_ref, live_ref, cot_live_ref, cos_t_ref,
    h_ref, gate_w_ref, cot_ref, count_ref, src_ref, cos_ref, sems,
):
    first = [pltpu.make_async_copy(src_hbm, src_ref, sems.at[8]), pltpu.make_async_copy(cos_hbm, cos_ref, sems.at[9])]
    copies = [
        pltpu.make_async_copy(ref, w_ref.at[pl.ds(64 * n, 64)], sems.at[n])
        for n, ref in enumerate((ws_hbm, wm_hbm, wt_hbm, wf_hbm))
    ]
    copies.append(pltpu.make_async_copy(h_hbm, h_ref, sems.at[4]))
    copies.append(pltpu.make_async_copy(gate_w_hbm, gate_w_ref, sems.at[5]))
    copies.append(pltpu.make_async_copy(cot_hbm, cot_ref, sems.at[6]))
    copies.append(pltpu.make_async_copy(count_hbm, count_ref, sems.at[7]))
    for copy in first + copies:
        copy.start()
    odd = odd_ref[0]
    rows = 256 // NDOM
    m = lax.broadcasted_iota(jnp.int32, (256, 1), 0)
    i = lax.broadcasted_iota(jnp.int32, (256, 256), 1)
    half = jnp.where(m < 128, 1 - odd, odd)
    m = m & 127
    want = (m // rows) * (2 * rows) + rows * half + m % rows
    perm = (i == want).astype(F32).astype(BF16)
    perm_ref[...] = perm
    for copy in first:
        copy.wait()
    src, cos = by_slot(src_ref, cos_ref)
    cos_t_ref[...] = cos
    low_base = jnp.where(odd == 1, CAP, CAP + GHOST)
    high_base = jnp.where(odd == 1, CAP + GHOST, CAP)
    row = jnp.where(
        src < GHOST,
        src + low_base,
        jnp.where(src >= CAP + GHOST, src - (CAP + GHOST) + high_base, src - GHOST),
    )
    near_row = row.astype(F32).astype(BF16)
    far_row = (row - CAP).astype(F32).astype(BF16)
    near_id = lax.broadcasted_iota(jnp.int32, (CAP, CAP), 0).astype(F32).astype(BF16)
    far_id = lax.broadcasted_iota(jnp.int32, (2 * GHOST, CAP), 0).astype(F32).astype(BF16)
    one, zero = jnp.ones((), BF16), jnp.zeros((), BF16)
    for k in range(ARITY):
        at = slice(k * CAP, (k + 1) * CAP)
        hot_ref[:CAP, at] = jnp.where(near_id == near_row[k : k + 1], one, zero)
        hot_ref[CAP:, at] = jnp.where(far_id == far_row[k : k + 1], one, zero)
    for copy in copies:
        copy.wait()
    live = live_row(count_ref[0])
    live_ref[...] = jnp.broadcast_to(live, (8, CAP))
    cot_live_ref[...] = cot_ref[...].astype(F32) * live
    h_t = h_ref[...].T
    w_t = w_ref[...]
    hp_ref[...] = dot(perm, h_t).astype(BF16)
    own = dot(w_t, h_t)
    own_ref[...] = own[128:]
    high, low = two_parts(own[:128])
    table = jnp.concatenate([high, low], axis=0)
    eye = lax.broadcasted_iota(jnp.int32, (64, 64), 0) == lax.broadcasted_iota(jnp.int32, (64, 64), 1)
    gate_w = jnp.sum(jnp.where(eye, gate_w_ref[...], 0.0), axis=1, keepdims=True)
    for k in range(ARITY):
        picked = dot(table, hot_ref[:CAP, k * CAP : (k + 1) * CAP])
        part_ref[k, 0:64] = picked[0:64] + picked[128:192] + (own[128:192] + gate_w * cos[k : k + 1])
        part_ref[k, 64:128] = picked[64:128] + picked[192:256]


def prep_stage(odd, count, *held):
    return pl.pallas_call(
        prep_kernel,
        out_shape=(
            stay((256, CAP), BF16),
            stay((256, 256), BF16),
            stay((256, 256), BF16),
            stay((128, CAP), F32),
            stay((EXT, ARITY * CAP), BF16),
            stay((ARITY, 128, CAP), F32),
            stay((8, CAP), F32),
            stay((64, CAP), F32),
            stay((16, CAP), F32),
        ),
        in_specs=[SMEM] + [HBM] * 10,
        out_specs=(VMEM,) * 9,
        scratch_shapes=[
            pltpu.VMEM((CAP, 256), BF16),
            pltpu.VMEM((1, 64), F32),
            pltpu.VMEM((64, CAP), BF16),
            pltpu.SMEM((1,), jnp.int32),
            pltpu.VMEM((24, 128), jnp.int32),
            pltpu.VMEM((24, 128), F32),
            pltpu.SemaphoreType.DMA((10,)),
        ],
        compiler_params=pltpu.CompilerParams(vmem_limit_bytes=24 << 20),
        name="prep_stage",
    )(odd, count, *(in_hbm(x) for x in held))


def angle_kernel(
    ga_ref, gb_ref, hp_ref, w_ref, perm_ref, own_ref, hot_ref, part_ref, live_ref, cot_live_ref, cos_ref,
    whole_ref, send_ref, keep_ref,
    pick_ref, sig_ref, both_ref, bonds_ref, slope_ref,
):
    w_t = w_ref[...]
    gh_t = jnp.concatenate([ga_ref[...], gb_ref[...]], axis=0).T
    high, low = two_parts(dot(w_t[:128], gh_t))
    table = jnp.concatenate([high, low], axis=1)
    gh_p = dot(perm_ref[...], gh_t).astype(BF16)
    for k in range(ARITY):
        far = hot_ref[CAP:, k * CAP : (k + 1) * CAP]
        pick_ref[k] = dot(table, jnp.concatenate([far, far], axis=0)) + part_ref[k]

    for at in (slice(0, 128), slice(128, 256)):
        live = live_ref[0:1, at]
        num = jnp.zeros((64, 128), F32)
        den = jnp.zeros((64, 128), F32)
        for k in range(ARITY):
            sig = sigmoid(pick_ref[k, 0:64, at])
            gate = sig * live
            num += gate * pick_ref[k, 64:128, at]
            den += gate
            sig_ref[k, :, at] = sig
        den = den + EPS
        agg = num / den
        z = own_ref[64:128, at] + agg
        s = sigmoid(z)
        dz = cot_live_ref[:, at] * (s * (1.0 + z * (1.0 - s)))
        dnum = dz / den
        dden = -(dnum * agg)
        bonds_ref[64:128, at] = dz.astype(BF16)
        slope_ref[0:64, at] = dnum
        slope_ref[64:128, at] = dden
    zero = jnp.zeros((64, 128), F32)
    dq2, dgw = [zero, zero], [zero, zero]
    acc = jnp.zeros((EXT, 128), F32)
    for first in range(0, ARITY, CHUNK):
        for n in (0, 1):
            at = slice(n * 128, (n + 1) * 128)
            live = live_ref[0:1, at]
            dnum = slope_ref[0:64, at]
            dden = slope_ref[64:128, at]
            for k in range(first, first + CHUNK):
                sig = sig_ref[k, :, at]
                gate = sig * live
                dgate = dnum * pick_ref[k, 64:128, at] + dden
                dpre = dgate * gate * (1.0 - sig)
                dq2[n] += dpre
                dgw[n] += dpre * cos_ref[k : k + 1, at]
                lane = slice(k * CAP + at.start, k * CAP + at.stop)
                both_ref[0:64, lane] = dpre.astype(BF16)
                both_ref[64:128, lane] = (gate * dnum).astype(BF16)
        lanes = slice(first * CAP, (first + CHUNK) * CAP)
        acc += dot(hot_ref[:, lanes], both_ref[:, lanes], 1, 1)
    dgw = jnp.concatenate(dgw, axis=1)
    bonds_ref[0:64] = jnp.concatenate(dq2, axis=1).astype(BF16)
    edge = acc.astype(BF16)
    bonds = bonds_ref[...].T
    full = jnp.concatenate([edge[:CAP], bonds], axis=1)
    edge_far = edge[CAP:]
    whole_ref[:, :CAP] = dot(full, w_t).astype(BF16).T
    whole_ref[:, CAP:] = dot(edge_far, w_t[:128]).astype(BF16).T
    grads = dot(hp_ref[...], full)
    grads = jnp.concatenate([grads[:, :128] + dot(gh_p, edge_far), grads[:, 128:]], axis=1)
    ones = jnp.ones((8, CAP), BF16)
    dgw_high, dgw_low = two_parts(dgw)
    gate = dot(ones, dgw_high, 1, 1) + dot(ones, dgw_low, 1, 1)
    keep_ref[0:128] = grads[128:256]
    keep_ref[128:136] = jnp.concatenate([gate, jnp.zeros((8, 192), F32)], axis=1)
    send_ref[0:128] = grads[0:128].astype(BF16)
    gate_high, gate_low = two_parts(gate)
    row = jnp.concatenate([gate_high, gate_low, jnp.zeros((8, 128), BF16)], axis=1)
    send_ref[128:144] = jnp.concatenate([row, row], axis=0)


def angle_stage(ga, gb, prepared):
    return pl.pallas_call(
        angle_kernel,
        out_shape=(
            stay((256, EXT), BF16),
            stay((144, 256), BF16),
            stay((136, 256), F32),
        ),
        in_specs=[VMEM] * 11,
        out_specs=(VMEM, VMEM, VMEM),
        scratch_shapes=[
            pltpu.VMEM((ARITY, 128, CAP), F32),
            pltpu.VMEM((ARITY, 64, CAP), F32),
            pltpu.VMEM((128, ARITY * CAP), BF16),
            pltpu.VMEM((128, CAP), BF16),
            pltpu.VMEM((128, CAP), F32),
        ],
        compiler_params=pltpu.CompilerParams(vmem_limit_bytes=24 << 20),
        name="angle_stage",
    )(in_vmem(ga), in_vmem(gb), *prepared)


def pair_kernel(keep_ref, recv_ref, out_ref):
    out_ref[:, :256] = (keep_ref[0:128] + recv_ref[0:128].astype(F32)).astype(BF16)
    row = recv_ref[128:144].astype(F32)[0:8]
    gate = keep_ref[128:136][:, 0:64] + row[:, 0:64] + row[:, 64:128]
    high, low = two_parts(gate)
    out_ref[:, 256:] = jnp.broadcast_to(jnp.concatenate([high, low], axis=1)[0:1], (128, 128))


def pair_stage(keep, recv):
    return pl.pallas_call(
        pair_kernel,
        out_shape=jax.ShapeDtypeStruct((128, 384), BF16),
        in_specs=[VMEM, VMEM],
        out_specs=VMEM,
        compiler_params=pltpu.CompilerParams(vmem_limit_bytes=24 << 20),
        name="pair_stage",
    )(keep, in_vmem(recv))


def last_kernel(slots_ref, source_ref, target_ref, message_ref, self_ref, gate_ref):
    total = jnp.sum(slots_ref[...].astype(F32), axis=0)
    source_ref[...] = total[:, 0:64]
    message_ref[...] = total[:, 64:128]
    target_ref[...] = total[:, 128:192]
    self_ref[...] = total[:, 192:256]
    gate_ref[...] = total[0:1, 256:320] + total[0:1, 320:384]


def last_stage(slots):
    rows = slots.shape[1]
    square = jax.ShapeDtypeStruct((rows, 64), F32)
    return pl.pallas_call(
        last_kernel,
        out_shape=(square, square, square, square, jax.ShapeDtypeStruct((1, 64), F32)),
        in_specs=[VMEM],
        out_specs=(VMEM,) * 5,
        compiler_params=pltpu.CompilerParams(vmem_limit_bytes=24 << 20),
        name="last_stage",
    )(in_vmem(slots))


def swap_core(x):
    return lax.ppermute(x, DOM, [(i, i ^ 1) for i in range(NDOM)])


def swap_chip(x):
    return lax.ppermute(x, DOM, [(i, (i + 1) % NDOM if i % 2 else (i - 1) % NDOM) for i in range(NDOM)])


def per_device(
    bond_feats,
    cotangent,
    bond_count,
    source,
    cosine,
    w_source,
    w_target,
    w_message,
    w_self,
    gate_angle,
):
    odd = lax.axis_index("dom_2").astype(jnp.int32)
    is_odd = odd == 1
    first, last = bond_feats[:GHOST], bond_feats[CAP - GHOST :]
    to_b, to_a = jnp.where(is_odd, last, first), jnp.where(is_odd, first, last)
    ghost_b = swap_chip(to_b)
    ghost_a = swap_core(to_a)
    prepared = prep_stage(
        odd.reshape(1),
        bond_count,
        source.reshape(24, 128),
        cosine.reshape(24, 128),
        bond_feats,
        w_source.T,
        w_message.T,
        w_target.T,
        w_self.T,
        gate_angle[None, :],
        cotangent.T,
    )
    whole, send, keep = angle_stage(ghost_a, ghost_b, prepared)
    tiles = lax.all_to_all(whole.reshape(4, 64, EXT), "wa", 0, 0, tiled=True)
    recv = swap_core(send)
    slots = pair_stage(keep, recv).reshape(NDOM // 2, 256 // NDOM, 384)
    slots = lax.all_to_all(slots, CHIP, 0, 0, tiled=True)
    summed = tiles.astype(F32).sum(axis=0)
    to_a, to_b = summed[:, CAP : CAP + GHOST], summed[:, CAP + GHOST :]
    back_b = swap_chip(to_b)
    back_a = swap_core(to_a)
    g_source, g_target, g_message, g_self, g_gate = last_stage(slots)

    total = summed[:, :CAP] + prepared[-2]
    to_first = jnp.where(is_odd, back_a, back_b)
    to_last = jnp.where(is_odd, back_b, back_a)
    added = jnp.concatenate([to_first, jnp.zeros((64, CAP - 2 * GHOST), F32), to_last], axis=1)
    bond_grad = (total + added).astype(BF16).T
    return (bond_grad, g_source, g_target, g_message, g_self, g_gate[0])


def solution(mesh):
    finer = Mesh(mesh.devices.reshape(8, 8, 2, mesh.shape["wa"]), ("dom_0", "dom_1", "dom_2", "wa"))
    return jax.shard_map(
        per_device,
        mesh=finer,
        in_specs=(
            P(DOM, None),
            P(DOM, "wa"),
            P(DOM),
            P(DOM),
            P(DOM),
            P(None, "wa"),
            P(None, "wa"),
            P(None, "wa"),
            P(None, "wa"),
            P("wa"),
        ),
        out_specs=(P(DOM, "wa"), P(DOM, "wa"), P(DOM, "wa"), P(DOM, "wa"), P(DOM, "wa"), P("wa")),
        check_vma=False,
    )
```

```python
import jax
import jax.numpy as jnp
from jax import lax
from jax.experimental import pallas as pl
from jax.experimental.pallas import tpu as pltpu
from jax.sharding import Mesh
from jax.sharding import PartitionSpec as P


ARITY = 12
CHUNK = 12
GHOST = 32
CAP = 256
EXT = CAP + 2 * GHOST
DOM = ("dom_0", "dom_1", "dom_2")
CHIP = ("dom_0", "dom_1")
NDOM = 128
EPS = 1e-06
F32 = jnp.float32
BF16 = jnp.bfloat16
VMEM = pl.BlockSpec(memory_space=pltpu.VMEM)
SMEM = pl.BlockSpec(memory_space=pltpu.SMEM)
HBM = pl.BlockSpec(memory_space=pltpu.HBM)


def dot(a, b, ca=1, cb=0):
    return lax.dot_general(a, b, (((ca,), (cb,)), ((), ())), preferred_element_type=F32)


def sigmoid(v):
    return 1.0 / (1.0 + jnp.exp(-v))


def two_parts(v):
    high = v.astype(BF16)
    return high, (v - high.astype(F32)).astype(BF16)


def in_vmem(x):
    return pltpu.with_memory_space_constraint(x, pltpu.VMEM)


def in_hbm(x):
    return pltpu.with_memory_space_constraint(x, pltpu.HBM)


def stay(shape, dtype):
    return pltpu.VMEM(shape, dtype)


def live_row(count):
    bond = lax.broadcasted_iota(jnp.int32, (1, CAP), 1)
    return ((bond < count - GHOST) | (bond >= CAP - GHOST)).astype(F32)


def by_slot(src_ref, cos_ref):
    def grouped(ref):
        return jnp.concatenate([ref[pl.ds(t, 8, stride=3), :] for t in range(3)], axis=1)

    cos = grouped(cos_ref)
    one, two = two_parts(cos)
    middle = EXT // 2
    src = (grouped(src_ref) - middle).astype(F32)
    parts = jnp.concatenate([src, one.astype(F32), two.astype(F32), jnp.zeros((8, 384), F32)], axis=0).astype(BF16)
    spot = lax.broadcasted_iota(jnp.int32, (384, CAP), 0)
    start = (lax.broadcasted_iota(jnp.int32, (1, CAP), 1) & 31) * ARITY
    inside = (spot >= start) & (spot < start + ARITY)
    slot = lax.broadcasted_iota(jnp.int32, (16, 384), 1) % ARITY
    slot = (slot == lax.broadcasted_iota(jnp.int32, (16, 384), 0)).astype(F32).astype(BF16)
    group = lax.broadcasted_iota(jnp.int32, (32, CAP), 0)
    wanted = lax.broadcasted_iota(jnp.int32, (32, CAP), 1) >> 5
    rows = []
    for n in range(3):
        pick = (group == wanted + 8 * n).astype(F32).astype(BF16)
        spread = jnp.where(inside, dot(parts, pick, 0, 0), 0.0).astype(BF16)
        rows.append(dot(slot, spread))
    return rows[0].astype(jnp.int32) + middle, rows[1] + rows[2]


def prep_kernel(
    odd_ref, count_ref, src_hbm, cos_hbm, h_hbm, ws_hbm, wm_hbm, wt_hbm, wf_hbm, gate_w_hbm, cot_hbm,
    h_t_ref, w_ref, own_ref, hot_ref, part_ref, live_ref, cot_live_ref, cos_t_ref,
    h_ref, gate_w_ref, cot_ref, src_ref, cos_ref, sems,
):
    first = [pltpu.make_async_copy(src_hbm, src_ref, sems.at[7]), pltpu.make_async_copy(cos_hbm, cos_ref, sems.at[8])]
    copies = [
        pltpu.make_async_copy(ref, w_ref.at[pl.ds(64 * n, 64)], sems.at[n])
        for n, ref in enumerate((ws_hbm, wm_hbm, wt_hbm, wf_hbm))
    ]
    copies.append(pltpu.make_async_copy(h_hbm, h_ref, sems.at[4]))
    copies.append(pltpu.make_async_copy(gate_w_hbm, gate_w_ref, sems.at[5]))
    copies.append(pltpu.make_async_copy(cot_hbm, cot_ref, sems.at[6]))
    for copy in first + copies:
        copy.start()
    odd = odd_ref[0]
    for copy in first:
        copy.wait()
    src, cos = by_slot(src_ref, cos_ref)
    cos_t_ref[...] = cos
    low_base = jnp.where(odd == 1, CAP, CAP + GHOST)
    high_base = jnp.where(odd == 1, CAP + GHOST, CAP)
    row = jnp.where(
        src < GHOST,
        src + low_base,
        jnp.where(src >= CAP + GHOST, src - (CAP + GHOST) + high_base, src - GHOST),
    )
    near_row = row.astype(F32).astype(BF16)
    far_row = (row - CAP).astype(F32).astype(BF16)
    near_id = lax.broadcasted_iota(jnp.int32, (CAP, CAP), 0).astype(F32).astype(BF16)
    far_id = lax.broadcasted_iota(jnp.int32, (2 * GHOST, CAP), 0).astype(F32).astype(BF16)
    one, zero = jnp.ones((), BF16), jnp.zeros((), BF16)
    for copy in copies:
        copy.wait()
    live = live_row(count_ref[0])
    live_ref[...] = jnp.broadcast_to(live, (8, CAP))
    cot_live_ref[...] = cot_ref[...].astype(F32) * live
    h_t = h_ref[...].T
    w_t = w_ref[...]
    h_t_ref[...] = h_t
    own = dot(w_t, h_t)
    own_ref[...] = own[128:]
    high, low = two_parts(own[:128])
    table = jnp.concatenate([high, low], axis=0)
    eye = lax.broadcasted_iota(jnp.int32, (64, 64), 0) == lax.broadcasted_iota(jnp.int32, (64, 64), 1)
    gate_w = jnp.sum(jnp.where(eye, gate_w_ref[...], 0.0), axis=1, keepdims=True)
    for k in range(ARITY):
        at = slice(k * CAP, (k + 1) * CAP)
        hot = jnp.where(near_id == near_row[k : k + 1], one, zero)
        hot_ref[:CAP, at] = hot
        hot_ref[CAP:, at] = jnp.where(far_id == far_row[k : k + 1], one, zero)
        picked = dot(table, hot)
        part_ref[k, 0:64] = picked[0:64] + picked[128:192] + (own[128:192] + gate_w * cos[k : k + 1])
        part_ref[k, 64:128] = picked[64:128] + picked[192:256]


def prep_stage(odd, count, *held):
    return pl.pallas_call(
        prep_kernel,
        out_shape=(
            stay((256, CAP), BF16),
            stay((256, 256), BF16),
            stay((128, CAP), F32),
            stay((EXT, ARITY * CAP), BF16),
            stay((ARITY, 128, CAP), F32),
            stay((8, CAP), F32),
            stay((64, CAP), F32),
            stay((16, CAP), F32),
        ),
        in_specs=[SMEM, SMEM] + [HBM] * 9,
        out_specs=(VMEM,) * 8,
        scratch_shapes=[
            pltpu.VMEM((CAP, 256), BF16),
            pltpu.VMEM((1, 64), F32),
            pltpu.VMEM((64, CAP), BF16),
            pltpu.VMEM((24, 128), jnp.int32),
            pltpu.VMEM((24, 128), F32),
            pltpu.SemaphoreType.DMA((9,)),
        ],
        compiler_params=pltpu.CompilerParams(vmem_limit_bytes=24 << 20),
        name="prep_stage",
    )(odd, count, *(in_hbm(x) for x in held))


def angle_kernel(
    ga_ref, gb_ref, w_ref, own_ref, hot_ref, part_ref, live_ref, cot_live_ref, cos_ref,
    whole_ref, full_ref, edge_ref, dgw_ref,
    pick_ref, sig_ref, bonds_ref, slope_ref,
):
    w_t = w_ref[...]
    gh_t = jnp.concatenate([ga_ref[...], gb_ref[...]], axis=0).T
    high, low = two_parts(dot(w_t[:128], gh_t))
    table = jnp.concatenate([high, low], axis=1)
    for k in range(ARITY):
        far = hot_ref[CAP:, k * CAP : (k + 1) * CAP]
        pick_ref[k] = dot(table, jnp.concatenate([far, far], axis=0)) + part_ref[k]

    for at in (slice(0, 128), slice(128, 256)):
        live = live_ref[0:1, at]
        num = jnp.zeros((64, 128), F32)
        den = jnp.zeros((64, 128), F32)
        for k in range(ARITY):
            sig = sigmoid(pick_ref[k, 0:64, at])
            gate = sig * live
            num += gate * pick_ref[k, 64:128, at]
            den += gate
            sig_ref[k, :, at] = sig
        den = den + EPS
        agg = num / den
        z = own_ref[64:128, at] + agg
        s = sigmoid(z)
        dz = cot_live_ref[:, at] * (s * (1.0 + z * (1.0 - s)))
        dnum = dz / den
        dden = -(dnum * agg)
        bonds_ref[64:128, at] = dz.astype(BF16)
        slope_ref[0:64, at] = dnum
        slope_ref[64:128, at] = dden
    zero = jnp.zeros((64, 128), F32)
    dq2, dgw = [zero, zero], [zero, zero]
    acc = jnp.zeros((EXT, 128), F32)
    for first in range(0, ARITY, CHUNK):
        chunk = []
        for k in range(first, first + CHUNK):
            dpre, dmsg = [], []
            for n in (0, 1):
                at = slice(n * 128, (n + 1) * 128)
                dnum = slope_ref[0:64, at]
                sig = sig_ref[k, :, at]
                gate = sig * live_ref[0:1, at]
                dgate = dnum * pick_ref[k, 64:128, at] + slope_ref[64:128, at]
                change = dgate * gate * (1.0 - sig)
                dq2[n] += change
                dgw[n] += change * cos_ref[k : k + 1, at]
                dpre.append(change.astype(BF16))
                dmsg.append((gate * dnum).astype(BF16))
            chunk.append(jnp.concatenate([jnp.concatenate(dpre, axis=1), jnp.concatenate(dmsg, axis=1)], axis=0))
        acc += dot(hot_ref[:, first * CAP : (first + CHUNK) * CAP], jnp.concatenate(chunk, axis=1), 1, 1)
    dgw_ref[...] = jnp.concatenate(dgw, axis=1)
    bonds_ref[0:64] = jnp.concatenate(dq2, axis=1).astype(BF16)
    edge = acc.astype(BF16)
    full = jnp.concatenate([edge[:CAP], bonds_ref[...].T], axis=1)
    edge_far = edge[CAP:]
    full_ref[...] = full
    edge_ref[...] = edge_far
    whole_ref[:, :CAP] = dot(full, w_t).astype(BF16).T
    whole_ref[:, CAP:] = dot(edge_far, w_t[:128]).astype(BF16).T


def angle_stage(ga, gb, *prepared):
    return pl.pallas_call(
        angle_kernel,
        out_shape=(
            stay((256, EXT), BF16),
            stay((CAP, 256), BF16),
            stay((2 * GHOST, 128), BF16),
            stay((64, CAP), F32),
        ),
        in_specs=[VMEM] * 9,
        out_specs=(VMEM,) * 4,
        scratch_shapes=[
            pltpu.VMEM((ARITY, 128, CAP), F32),
            pltpu.VMEM((ARITY, 64, CAP), F32),
            pltpu.VMEM((128, CAP), BF16),
            pltpu.VMEM((128, CAP), F32),
        ],
        compiler_params=pltpu.CompilerParams(vmem_limit_bytes=24 << 20),
        name="angle_stage",
    )(in_vmem(ga), in_vmem(gb), *(in_vmem(x) for x in prepared))


def grads_kernel(odd_ref, ga_ref, gb_ref, h_t_ref, full_ref, edge_ref, dgw_ref, send_ref, keep_ref):
    odd = odd_ref[0]
    rows = 256 // NDOM
    m = lax.broadcasted_iota(jnp.int32, (256, 1), 0)
    i = lax.broadcasted_iota(jnp.int32, (256, 256), 1)
    half = jnp.where(m < 128, 1 - odd, odd)
    m = m & 127
    want = (m // rows) * (2 * rows) + rows * half + m % rows
    perm = (i == want).astype(F32).astype(BF16)
    full = full_ref[...]
    gh_t = jnp.concatenate([ga_ref[...], gb_ref[...]], axis=0).T
    own = dot(h_t_ref[...], full)
    own = jnp.concatenate([own[:, :128] + dot(gh_t, edge_ref[...]), own[:, 128:]], axis=1)
    high, low = two_parts(own)
    send_ref[0:128] = dot(perm[:128], high).astype(BF16)
    keep_ref[0:128] = dot(perm[128:], high) + dot(perm[128:], low)
    ones = jnp.ones((8, CAP), BF16)
    dgw_high, dgw_low = two_parts(dgw_ref[...])
    gate = dot(ones, dgw_high, 1, 1) + dot(ones, dgw_low, 1, 1)
    keep_ref[128:136] = jnp.concatenate([gate, jnp.zeros((8, 192), F32)], axis=1)
    gate_high, gate_low = two_parts(gate)
    row = jnp.concatenate([gate_high, gate_low, jnp.zeros((8, 128), BF16)], axis=1)
    send_ref[128:144] = jnp.concatenate([row, row], axis=0)


def grads_stage(odd, ga, gb, *found):
    return pl.pallas_call(
        grads_kernel,
        out_shape=(stay((144, 256), BF16), stay((136, 256), F32)),
        in_specs=[SMEM] + [VMEM] * 6,
        out_specs=(VMEM, VMEM),
        compiler_params=pltpu.CompilerParams(vmem_limit_bytes=24 << 20),
        name="grads_stage",
    )(odd, in_vmem(ga), in_vmem(gb), *found)


def pair_kernel(keep_ref, recv_ref, out_ref):
    out_ref[:, :256] = (keep_ref[0:128] + recv_ref[0:128].astype(F32)).astype(BF16)
    row = recv_ref[128:144].astype(F32)[0:8]
    gate = keep_ref[128:136][:, 0:64] + row[:, 0:64] + row[:, 64:128]
    high, low = two_parts(gate)
    out_ref[:, 256:] = jnp.broadcast_to(jnp.concatenate([high, low], axis=1)[0:1], (128, 128))


def pair_stage(keep, recv):
    return pl.pallas_call(
        pair_kernel,
        out_shape=jax.ShapeDtypeStruct((128, 384), BF16),
        in_specs=[VMEM, VMEM],
        out_specs=VMEM,
        compiler_params=pltpu.CompilerParams(vmem_limit_bytes=24 << 20),
        name="pair_stage",
    )(keep, in_vmem(recv))


def last_kernel(slots_ref, source_ref, target_ref, message_ref, self_ref, gate_ref):
    total = jnp.sum(slots_ref[...].astype(F32), axis=0)
    source_ref[...] = total[:, 0:64]
    message_ref[...] = total[:, 64:128]
    target_ref[...] = total[:, 128:192]
    self_ref[...] = total[:, 192:256]
    gate_ref[...] = total[0:1, 256:320] + total[0:1, 320:384]


def last_stage(slots):
    rows = slots.shape[1]
    square = jax.ShapeDtypeStruct((rows, 64), F32)
    return pl.pallas_call(
        last_kernel,
        out_shape=(square, square, square, square, jax.ShapeDtypeStruct((1, 64), F32)),
        in_specs=[VMEM],
        out_specs=(VMEM,) * 5,
        compiler_params=pltpu.CompilerParams(vmem_limit_bytes=24 << 20),
        name="last_stage",
    )(in_vmem(slots))


def swap_core(x):
    return lax.ppermute(x, DOM, [(i, i ^ 1) for i in range(NDOM)])


def swap_chip(x):
    return lax.ppermute(x, DOM, [(i, (i + 1) % NDOM if i % 2 else (i - 1) % NDOM) for i in range(NDOM)])


def per_device(
    bond_feats,
    cotangent,
    bond_count,
    source,
    cosine,
    w_source,
    w_target,
    w_message,
    w_self,
    gate_angle,
):
    odd = lax.axis_index("dom_2").astype(jnp.int32)
    is_odd = odd == 1
    first, last = bond_feats[:GHOST], bond_feats[CAP - GHOST :]
    to_b, to_a = jnp.where(is_odd, last, first), jnp.where(is_odd, first, last)
    ghost_b = swap_chip(to_b)
    ghost_a = swap_core(to_a)
    odd = odd.reshape(1)
    h_t, *prepared = prep_stage(
        odd,
        bond_count,
        source.reshape(24, 128),
        cosine.reshape(24, 128),
        bond_feats,
        w_source.T,
        w_message.T,
        w_target.T,
        w_self.T,
        gate_angle[None, :],
        cotangent.T,
    )
    whole, *found = angle_stage(ghost_a, ghost_b, *prepared)
    tiles = lax.all_to_all(whole.reshape(4, 64, EXT), "wa", 0, 0, tiled=True)
    send, keep = grads_stage(odd, ghost_a, ghost_b, h_t, *found)
    recv = swap_core(send)
    slots = pair_stage(keep, recv).reshape(NDOM // 2, 256 // NDOM, 384)
    slots = lax.all_to_all(slots, CHIP, 0, 0, tiled=True)
    summed = tiles.astype(F32).sum(axis=0)
    to_a, to_b = summed[:, CAP : CAP + GHOST], summed[:, CAP + GHOST :]
    back_b = swap_chip(to_b)
    back_a = swap_core(to_a)
    g_source, g_target, g_message, g_self, g_gate = last_stage(slots)

    total = summed[:, :CAP] + prepared[-2]
    to_first = jnp.where(is_odd, back_a, back_b)
    to_last = jnp.where(is_odd, back_b, back_a)
    added = jnp.concatenate([to_first, jnp.zeros((64, CAP - 2 * GHOST), F32), to_last], axis=1)
    bond_grad = (total + added).astype(BF16).T
    return (bond_grad, g_source, g_target, g_message, g_self, g_gate[0])


def solution(mesh):
    finer = Mesh(mesh.devices.reshape(8, 8, 2, mesh.shape["wa"]), ("dom_0", "dom_1", "dom_2", "wa"))
    return jax.shard_map(
        per_device,
        mesh=finer,
        in_specs=(
            P(DOM, None),
            P(DOM, "wa"),
            P(DOM),
            P(DOM),
            P(DOM),
            P(None, "wa"),
            P(None, "wa"),
            P(None, "wa"),
            P(None, "wa"),
            P("wa"),
        ),
        out_specs=(P(DOM, "wa"), P(DOM, "wa"), P(DOM, "wa"), P(DOM, "wa"), P(DOM, "wa"), P("wa")),
        check_vma=False,
    )
```

```python
import jax
import jax.numpy as jnp
from jax import lax
from jax.experimental import pallas as pl
from jax.experimental.pallas import tpu as pltpu
from jax.sharding import Mesh
from jax.sharding import PartitionSpec as P


ARITY = 12
CHUNK = 12
GHOST = 32
CAP = 256
EXT = CAP + 2 * GHOST
DOM = ("dom_0", "dom_1", "dom_2")
CHIP = ("dom_0", "dom_1")
NDOM = 128
EPS = 1e-06
F32 = jnp.float32
BF16 = jnp.bfloat16
VMEM = pl.BlockSpec(memory_space=pltpu.VMEM)
SMEM = pl.BlockSpec(memory_space=pltpu.SMEM)
HBM = pl.BlockSpec(memory_space=pltpu.HBM)


def dot(a, b, ca=1, cb=0):
    return lax.dot_general(a, b, (((ca,), (cb,)), ((), ())), preferred_element_type=F32)


def sigmoid(v):
    return 1.0 / (1.0 + jnp.exp(-v))


def two_parts(v):
    high = v.astype(BF16)
    return high, (v - high.astype(F32)).astype(BF16)


def in_vmem(x):
    return pltpu.with_memory_space_constraint(x, pltpu.VMEM)


def in_hbm(x):
    return pltpu.with_memory_space_constraint(x, pltpu.HBM)


def stay(shape, dtype):
    return pltpu.VMEM(shape, dtype)


def live_row(count):
    bond = lax.broadcasted_iota(jnp.int32, (1, CAP), 1)
    return ((bond < count - GHOST) | (bond >= CAP - GHOST)).astype(F32)


def by_slot(src_ref, cos_ref):
    def grouped(ref):
        return jnp.concatenate([ref[pl.ds(t, 8, stride=3), :] for t in range(3)], axis=1)

    cos = grouped(cos_ref)
    one, two = two_parts(cos)
    middle = EXT // 2
    src = (grouped(src_ref) - middle).astype(F32)
    parts = jnp.concatenate([src, one.astype(F32), two.astype(F32), jnp.zeros((8, 384), F32)], axis=0).astype(BF16)
    spot = lax.broadcasted_iota(jnp.int32, (384, CAP), 0)
    start = (lax.broadcasted_iota(jnp.int32, (1, CAP), 1) & 31) * ARITY
    inside = (spot >= start) & (spot < start + ARITY)
    slot = lax.broadcasted_iota(jnp.int32, (16, 384), 1) % ARITY
    slot = (slot == lax.broadcasted_iota(jnp.int32, (16, 384), 0)).astype(F32).astype(BF16)
    group = lax.broadcasted_iota(jnp.int32, (32, CAP), 0)
    wanted = lax.broadcasted_iota(jnp.int32, (32, CAP), 1) >> 5
    rows = []
    for n in range(3):
        pick = (group == wanted + 8 * n).astype(F32).astype(BF16)
        spread = jnp.where(inside, dot(parts, pick, 0, 0), 0.0).astype(BF16)
        rows.append(dot(slot, spread))
    return rows[0].astype(jnp.int32) + middle, rows[1] + rows[2]


def prep_kernel(
    odd_ref, count_ref, src_hbm, cos_hbm, h_hbm, ws_hbm, wm_hbm, wt_hbm, wf_hbm, gate_w_hbm, cot_hbm,
    h_t_ref, w_ref, own_ref, hot_ref, part_ref, live_ref, cot_live_ref, cos_t_ref,
    h_ref, gate_w_ref, cot_ref, src_ref, cos_ref, sems,
):
    first = [pltpu.make_async_copy(src_hbm, src_ref, sems.at[7]), pltpu.make_async_copy(cos_hbm, cos_ref, sems.at[8])]
    copies = [
        pltpu.make_async_copy(ref, w_ref.at[pl.ds(64 * n, 64)], sems.at[n])
        for n, ref in enumerate((ws_hbm, wm_hbm, wt_hbm, wf_hbm))
    ]
    copies.append(pltpu.make_async_copy(h_hbm, h_ref, sems.at[4]))
    copies.append(pltpu.make_async_copy(gate_w_hbm, gate_w_ref, sems.at[5]))
    copies.append(pltpu.make_async_copy(cot_hbm, cot_ref, sems.at[6]))
    for copy in first + copies:
        copy.start()
    odd = odd_ref[0]
    for copy in first + copies:
        copy.wait()
    src, cos = by_slot(src_ref, cos_ref)
    cos_t_ref[...] = cos
    low_base = jnp.where(odd == 1, CAP, CAP + GHOST)
    high_base = jnp.where(odd == 1, CAP + GHOST, CAP)
    row = jnp.where(
        src < GHOST,
        src + low_base,
        jnp.where(src >= CAP + GHOST, src - (CAP + GHOST) + high_base, src - GHOST),
    )
    near_row = row.astype(F32).astype(BF16)
    far_row = (row - CAP).astype(F32).astype(BF16)
    near_id = lax.broadcasted_iota(jnp.int32, (CAP, CAP), 0).astype(F32).astype(BF16)
    far_id = lax.broadcasted_iota(jnp.int32, (2 * GHOST, CAP), 0).astype(F32).astype(BF16)
    one, zero = jnp.ones((), BF16), jnp.zeros((), BF16)
    live = live_row(count_ref[0])
    live_ref[...] = jnp.broadcast_to(live, (8, CAP))
    cot_live_ref[...] = cot_ref[...].astype(F32) * live
    h_t = h_ref[...].T
    w_t = w_ref[...]
    h_t_ref[...] = h_t
    own = dot(w_t, h_t)
    own_ref[...] = own[128:]
    high, low = two_parts(own[:128])
    table = jnp.concatenate([high, low], axis=0)
    eye = lax.broadcasted_iota(jnp.int32, (64, 64), 0) == lax.broadcasted_iota(jnp.int32, (64, 64), 1)
    gate_w = jnp.sum(jnp.where(eye, gate_w_ref[...], 0.0), axis=1, keepdims=True)
    for k in range(ARITY):
        at = slice(k * CAP, (k + 1) * CAP)
        hot = jnp.where(near_id == near_row[k : k + 1], one, zero)
        hot_ref[:CAP, at] = hot
        hot_ref[CAP:, at] = jnp.where(far_id == far_row[k : k + 1], one, zero)
        picked = dot(table, hot)
        part_ref[k, 0:64] = picked[0:64] + picked[128:192] + (own[128:192] + gate_w * cos[k : k + 1])
        part_ref[k, 64:128] = picked[64:128] + picked[192:256]


def prep_stage(odd, count, *held):
    return pl.pallas_call(
        prep_kernel,
        out_shape=(
            stay((256, CAP), BF16),
            stay((256, 256), BF16),
            stay((128, CAP), F32),
            stay((EXT, ARITY * CAP), BF16),
            stay((ARITY, 128, CAP), F32),
            stay((8, CAP), F32),
            stay((64, CAP), F32),
            stay((16, CAP), F32),
        ),
        in_specs=[SMEM, SMEM] + [HBM] * 9,
        out_specs=(VMEM,) * 8,
        scratch_shapes=[
            pltpu.VMEM((CAP, 256), BF16),
            pltpu.VMEM((1, 64), F32),
            pltpu.VMEM((64, CAP), BF16),
            pltpu.VMEM((24, 128), jnp.int32),
            pltpu.VMEM((24, 128), F32),
            pltpu.SemaphoreType.DMA((9,)),
        ],
        compiler_params=pltpu.CompilerParams(vmem_limit_bytes=24 << 20),
        name="prep_stage",
    )(odd, count, *(in_hbm(x) for x in held))


def angle_kernel(
    ga_ref, gb_ref, w_ref, own_ref, hot_ref, part_ref, live_ref, cot_live_ref, cos_ref,
    whole_ref, full_ref, edge_ref, dgw_ref,
    pick_ref, sig_ref, bonds_ref, slope_ref,
):
    w_t = w_ref[...]
    gh_t = jnp.concatenate([ga_ref[...], gb_ref[...]], axis=0).T
    high, low = two_parts(dot(w_t[:128], gh_t))
    table = jnp.concatenate([high, low], axis=1)
    for k in range(ARITY):
        far = hot_ref[CAP:, k * CAP : (k + 1) * CAP]
        pick_ref[k] = dot(table, jnp.concatenate([far, far], axis=0)) + part_ref[k]

    for at in (slice(0, 128), slice(128, 256)):
        live = live_ref[0:1, at]
        num = jnp.zeros((64, 128), F32)
        den = jnp.zeros((64, 128), F32)
        for k in range(ARITY):
            sig = sigmoid(pick_ref[k, 0:64, at])
            gate = sig * live
            num += gate * pick_ref[k, 64:128, at]
            den += gate
            sig_ref[k, :, at] = sig
        den = den + EPS
        agg = num / den
        z = own_ref[64:128, at] + agg
        s = sigmoid(z)
        dz = cot_live_ref[:, at] * (s * (1.0 + z * (1.0 - s)))
        dnum = dz / den
        dden = -(dnum * agg)
        bonds_ref[64:128, at] = dz.astype(BF16)
        slope_ref[0:64, at] = dnum
        slope_ref[64:128, at] = dden
    zero = jnp.zeros((64, 128), F32)
    dq2, dgw = [zero, zero], [zero, zero]
    acc = jnp.zeros((EXT, 128), F32)
    for first in range(0, ARITY, CHUNK):
        chunk = []
        for k in range(first, first + CHUNK):
            dpre, dmsg = [], []
            for n in (0, 1):
                at = slice(n * 128, (n + 1) * 128)
                dnum = slope_ref[0:64, at]
                sig = sig_ref[k, :, at]
                gate = sig * live_ref[0:1, at]
                dgate = dnum * pick_ref[k, 64:128, at] + slope_ref[64:128, at]
                change = dgate * gate * (1.0 - sig)
                dq2[n] += change
                dgw[n] += change * cos_ref[k : k + 1, at]
                dpre.append(change.astype(BF16))
                dmsg.append((gate * dnum).astype(BF16))
            chunk.append(jnp.concatenate([jnp.concatenate(dpre, axis=1), jnp.concatenate(dmsg, axis=1)], axis=0))
        acc += dot(hot_ref[:, first * CAP : (first + CHUNK) * CAP], jnp.concatenate(chunk, axis=1), 1, 1)
    dgw_ref[...] = jnp.concatenate(dgw, axis=1)
    bonds_ref[0:64] = jnp.concatenate(dq2, axis=1).astype(BF16)
    edge = acc.astype(BF16)
    full = jnp.concatenate([edge[:CAP], bonds_ref[...].T], axis=1)
    edge_far = edge[CAP:]
    full_ref[...] = full
    edge_ref[...] = edge_far
    whole_ref[:, :CAP] = dot(full, w_t).astype(BF16).T
    whole_ref[:, CAP:] = dot(edge_far, w_t[:128]).astype(BF16).T


def angle_stage(ga, gb, *prepared):
    return pl.pallas_call(
        angle_kernel,
        out_shape=(
            stay((256, EXT), BF16),
            stay((CAP, 256), BF16),
            stay((2 * GHOST, 128), BF16),
            stay((64, CAP), F32),
        ),
        in_specs=[VMEM] * 9,
        out_specs=(VMEM,) * 4,
        scratch_shapes=[
            pltpu.VMEM((ARITY, 128, CAP), F32),
            pltpu.VMEM((ARITY, 64, CAP), F32),
            pltpu.VMEM((128, CAP), BF16),
            pltpu.VMEM((128, CAP), F32),
        ],
        compiler_params=pltpu.CompilerParams(vmem_limit_bytes=24 << 20),
        name="angle_stage",
    )(in_vmem(ga), in_vmem(gb), *(in_vmem(x) for x in prepared))


def grads_kernel(odd_ref, ga_ref, gb_ref, h_t_ref, full_ref, edge_ref, dgw_ref, send_ref, keep_ref):
    odd = odd_ref[0]
    rows = 256 // NDOM
    m = lax.broadcasted_iota(jnp.int32, (256, 1), 0)
    i = lax.broadcasted_iota(jnp.int32, (256, 256), 1)
    half = jnp.where(m < 128, 1 - odd, odd)
    m = m & 127
    want = (m // rows) * (2 * rows) + rows * half + m % rows
    perm = (i == want).astype(F32).astype(BF16)
    full = full_ref[...]
    gh_t = jnp.concatenate([ga_ref[...], gb_ref[...]], axis=0).T
    own = dot(h_t_ref[...], full)
    own = jnp.concatenate([own[:, :128] + dot(gh_t, edge_ref[...]), own[:, 128:]], axis=1)
    high, low = two_parts(own)
    send_ref[0:128] = dot(perm[:128], high).astype(BF16)
    keep_ref[0:128] = dot(perm[128:], high) + dot(perm[128:], low)
    ones = jnp.ones((8, CAP), BF16)
    dgw_high, dgw_low = two_parts(dgw_ref[...])
    gate = dot(ones, dgw_high, 1, 1) + dot(ones, dgw_low, 1, 1)
    keep_ref[128:136] = jnp.concatenate([gate, jnp.zeros((8, 192), F32)], axis=1)
    gate_high, gate_low = two_parts(gate)
    row = jnp.concatenate([gate_high, gate_low, jnp.zeros((8, 128), BF16)], axis=1)
    send_ref[128:144] = jnp.concatenate([row, row], axis=0)


def grads_stage(odd, ga, gb, *found):
    return pl.pallas_call(
        grads_kernel,
        out_shape=(stay((144, 256), BF16), stay((136, 256), F32)),
        in_specs=[SMEM] + [VMEM] * 6,
        out_specs=(VMEM, VMEM),
        compiler_params=pltpu.CompilerParams(vmem_limit_bytes=24 << 20),
        name="grads_stage",
    )(odd, in_vmem(ga), in_vmem(gb), *found)


def pair_kernel(keep_ref, recv_ref, out_ref):
    row = recv_ref[128:144].astype(F32)[0:8]
    gate = keep_ref[128:136][:, 0:64] + row[:, 0:64] + row[:, 64:128]
    high, low = two_parts(gate)
    tail = jnp.broadcast_to(jnp.concatenate([high, low], axis=1)[0:1], (128, 128))
    total = (keep_ref[0:128] + recv_ref[0:128].astype(F32)).astype(BF16)
    out_ref[...] = jnp.concatenate([total, tail], axis=1).reshape(out_ref.shape)


def pair_stage(keep, recv):
    return pl.pallas_call(
        pair_kernel,
        out_shape=stay((NDOM // 2, 256 // NDOM, 384), BF16),
        in_specs=[VMEM, VMEM],
        out_specs=VMEM,
        compiler_params=pltpu.CompilerParams(vmem_limit_bytes=24 << 20),
        name="pair_stage",
    )(keep, in_vmem(recv))


def last_kernel(slots_ref, source_ref, target_ref, message_ref, self_ref, gate_ref):
    total = jnp.sum(slots_ref[...].astype(F32), axis=0)
    source_ref[...] = total[:, 0:64]
    message_ref[...] = total[:, 64:128]
    target_ref[...] = total[:, 128:192]
    self_ref[...] = total[:, 192:256]
    gate_ref[...] = total[0:1, 256:320] + total[0:1, 320:384]


def last_stage(slots):
    rows = slots.shape[1]
    square = jax.ShapeDtypeStruct((rows, 64), F32)
    return pl.pallas_call(
        last_kernel,
        out_shape=(square, square, square, square, jax.ShapeDtypeStruct((1, 64), F32)),
        in_specs=[VMEM],
        out_specs=(VMEM,) * 5,
        compiler_params=pltpu.CompilerParams(vmem_limit_bytes=24 << 20),
        name="last_stage",
    )(in_vmem(slots))


def swap_core(x):
    return lax.ppermute(x, DOM, [(i, i ^ 1) for i in range(NDOM)])


def swap_chip(x):
    return lax.ppermute(x, DOM, [(i, (i + 1) % NDOM if i % 2 else (i - 1) % NDOM) for i in range(NDOM)])


def per_device(
    bond_feats,
    cotangent,
    bond_count,
    source,
    cosine,
    w_source,
    w_target,
    w_message,
    w_self,
    gate_angle,
):
    odd = lax.axis_index("dom_2").astype(jnp.int32)
    is_odd = odd == 1
    first, last = bond_feats[:GHOST], bond_feats[CAP - GHOST :]
    to_b, to_a = jnp.where(is_odd, last, first), jnp.where(is_odd, first, last)
    ghost_b = swap_chip(to_b)
    ghost_a = swap_core(to_a)
    odd = odd.reshape(1)
    h_t, *prepared = prep_stage(
        odd,
        bond_count,
        source.reshape(24, 128),
        cosine.reshape(24, 128),
        bond_feats,
        w_source.T,
        w_message.T,
        w_target.T,
        w_self.T,
        gate_angle[None, :],
        cotangent.T,
    )
    whole, *found = angle_stage(ghost_a, ghost_b, *prepared)
    tiles = lax.all_to_all(whole.reshape(4, 64, EXT), "wa", 0, 0, tiled=True)
    send, keep = grads_stage(odd, ghost_a, ghost_b, h_t, *found)
    recv = swap_core(send)
    slots = pair_stage(keep, recv)
    slots = lax.all_to_all(slots, CHIP, 0, 0, tiled=True)
    summed = tiles.astype(F32).sum(axis=0)
    to_a, to_b = summed[:, CAP : CAP + GHOST], summed[:, CAP + GHOST :]
    back_b = swap_chip(to_b)
    back_a = swap_core(to_a)
    g_source, g_target, g_message, g_self, g_gate = last_stage(slots)

    total = summed[:, :CAP] + prepared[-2]
    to_first = jnp.where(is_odd, back_a, back_b)
    to_last = jnp.where(is_odd, back_b, back_a)
    added = jnp.concatenate([to_first, jnp.zeros((64, CAP - 2 * GHOST), F32), to_last], axis=1)
    bond_grad = (total + added).astype(BF16).T
    return (bond_grad, g_source, g_target, g_message, g_self, g_gate[0])


def solution(mesh):
    finer = Mesh(mesh.devices.reshape(8, 8, 2, mesh.shape["wa"]), ("dom_0", "dom_1", "dom_2", "wa"))
    return jax.shard_map(
        per_device,
        mesh=finer,
        in_specs=(
            P(DOM, None),
            P(DOM, "wa"),
            P(DOM),
            P(DOM),
            P(DOM),
            P(None, "wa"),
            P(None, "wa"),
            P(None, "wa"),
            P(None, "wa"),
            P("wa"),
        ),
        out_specs=(P(DOM, "wa"), P(DOM, "wa"), P(DOM, "wa"), P(DOM, "wa"), P(DOM, "wa"), P("wa")),
        check_vma=False,
    )
```

```python
import jax
import jax.numpy as jnp
from jax import lax
from jax.experimental import pallas as pl
from jax.experimental.pallas import tpu as pltpu
from jax.sharding import Mesh
from jax.sharding import PartitionSpec as P


ARITY = 12
CHUNK = 12
GHOST = 32
CAP = 256
EXT = CAP + 2 * GHOST
DOM = ("dom_0", "dom_1", "dom_2")
CHIP = ("dom_0", "dom_1")
NDOM = 128
EPS = 1e-06
F32 = jnp.float32
BF16 = jnp.bfloat16
VMEM = pl.BlockSpec(memory_space=pltpu.VMEM)
SMEM = pl.BlockSpec(memory_space=pltpu.SMEM)
HBM = pl.BlockSpec(memory_space=pltpu.HBM)


def dot(a, b, ca=1, cb=0):
    return lax.dot_general(a, b, (((ca,), (cb,)), ((), ())), preferred_element_type=F32)


def sigmoid(v):
    return 1.0 / (1.0 + jnp.exp(-v))


def two_parts(v):
    high = v.astype(BF16)
    return high, (v - high.astype(F32)).astype(BF16)


def in_vmem(x):
    return pltpu.with_memory_space_constraint(x, pltpu.VMEM)


def in_hbm(x):
    return pltpu.with_memory_space_constraint(x, pltpu.HBM)


def stay(shape, dtype):
    return pltpu.VMEM(shape, dtype)


def live_row(count):
    bond = lax.broadcasted_iota(jnp.int32, (1, CAP), 1)
    return ((bond < count - GHOST) | (bond >= CAP - GHOST)).astype(F32)


def front_kernel(
    odd_ref, src_hbm, cos_hbm, h_hbm, ws_hbm, wm_hbm, wt_hbm, wf_hbm, gate_w_hbm, cot_hbm,
    to_a_ref, to_b_ref, src_ref, cos_ref, h_ref, w_ref, gate_w_ref, cot_ref,
    sems,
):
    odd = odd_ref[0]
    at_a = pl.multiple_of((1 - odd) * (CAP - GHOST), GHOST)
    at_b = pl.multiple_of(odd * (CAP - GHOST), GHOST)
    pairs = [
        (h_hbm.at[pl.ds(at_b, GHOST)], to_b_ref),
        (h_hbm.at[pl.ds(at_a, GHOST)], to_a_ref),
        (src_hbm, src_ref),
        (cos_hbm, cos_ref),
        (h_hbm, h_ref),
        (gate_w_hbm, gate_w_ref),
        (cot_hbm, cot_ref),
    ]
    for n, ref in enumerate((ws_hbm, wm_hbm, wt_hbm, wf_hbm)):
        pairs.append((ref, w_ref.at[pl.ds(64 * n, 64)]))
    copies = [pltpu.make_async_copy(a, b, sems.at[n]) for n, (a, b) in enumerate(pairs)]
    for copy in copies:
        copy.start()
    for copy in copies:
        copy.wait()


def front_stage(odd, *held):
    return pl.pallas_call(
        front_kernel,
        out_shape=(
            stay((GHOST, 256), BF16),
            stay((GHOST, 256), BF16),
            stay((24, 128), jnp.int32),
            stay((24, 128), F32),
            stay((CAP, 256), BF16),
            stay((256, 256), BF16),
            stay((1, 64), F32),
            stay((64, CAP), BF16),
        ),
        in_specs=[SMEM] + [HBM] * 9,
        out_specs=(VMEM,) * 8,
        scratch_shapes=[pltpu.SemaphoreType.DMA((11,))],
        compiler_params=pltpu.CompilerParams(vmem_limit_bytes=24 << 20),
        name="front_stage",
    )(odd, *(in_hbm(x) for x in held))


def by_slot(src_ref, cos_ref):
    def grouped(ref):
        return jnp.concatenate([ref[pl.ds(t, 8, stride=3), :] for t in range(3)], axis=1)

    cos = grouped(cos_ref)
    one, two = two_parts(cos)
    middle = EXT // 2
    src = (grouped(src_ref) - middle).astype(F32)
    parts = jnp.concatenate([src, one.astype(F32), two.astype(F32), jnp.zeros((8, 384), F32)], axis=0).astype(BF16)
    spot = lax.broadcasted_iota(jnp.int32, (384, CAP), 0)
    start = (lax.broadcasted_iota(jnp.int32, (1, CAP), 1) & 31) * ARITY
    inside = (spot >= start) & (spot < start + ARITY)
    slot = lax.broadcasted_iota(jnp.int32, (16, 384), 1) % ARITY
    slot = (slot == lax.broadcasted_iota(jnp.int32, (16, 384), 0)).astype(F32).astype(BF16)
    group = lax.broadcasted_iota(jnp.int32, (32, CAP), 0)
    wanted = lax.broadcasted_iota(jnp.int32, (32, CAP), 1) >> 5
    rows = []
    for n in range(3):
        pick = (group == wanted + 8 * n).astype(F32).astype(BF16)
        spread = jnp.where(inside, dot(parts, pick, 0, 0), 0.0).astype(BF16)
        rows.append(dot(slot, spread))
    return rows[0].astype(jnp.int32) + middle, rows[1] + rows[2]


def prep_kernel(
    odd_ref, count_ref, src_ref, cos_ref, h_ref, w_ref, gate_w_ref, cot_ref,
    h_t_ref, own_ref, hot_ref, part_ref, live_ref, cot_live_ref, cos_t_ref,
):
    odd = odd_ref[0]
    src, cos = by_slot(src_ref, cos_ref)
    cos_t_ref[...] = cos
    low_base = jnp.where(odd == 1, CAP, CAP + GHOST)
    high_base = jnp.where(odd == 1, CAP + GHOST, CAP)
    row = jnp.where(
        src < GHOST,
        src + low_base,
        jnp.where(src >= CAP + GHOST, src - (CAP + GHOST) + high_base, src - GHOST),
    )
    near_row = row.astype(F32).astype(BF16)
    far_row = (row - CAP).astype(F32).astype(BF16)
    near_id = lax.broadcasted_iota(jnp.int32, (CAP, CAP), 0).astype(F32).astype(BF16)
    far_id = lax.broadcasted_iota(jnp.int32, (2 * GHOST, CAP), 0).astype(F32).astype(BF16)
    one, zero = jnp.ones((), BF16), jnp.zeros((), BF16)
    live = live_row(count_ref[0])
    live_ref[...] = jnp.broadcast_to(live, (8, CAP))
    cot_live_ref[...] = cot_ref[...].astype(F32) * live
    h_t = h_ref[...].T
    w_t = w_ref[...]
    h_t_ref[...] = h_t
    own = dot(w_t, h_t)
    own_ref[...] = own[128:]
    high, low = two_parts(own[:128])
    table = jnp.concatenate([high, low], axis=0)
    eye = lax.broadcasted_iota(jnp.int32, (64, 64), 0) == lax.broadcasted_iota(jnp.int32, (64, 64), 1)
    gate_w = jnp.sum(jnp.where(eye, gate_w_ref[...], 0.0), axis=1, keepdims=True)
    for k in range(ARITY):
        at = slice(k * CAP, (k + 1) * CAP)
        hot = jnp.where(near_id == near_row[k : k + 1], one, zero)
        hot_ref[:CAP, at] = hot
        hot_ref[CAP:, at] = jnp.where(far_id == far_row[k : k + 1], one, zero)
        picked = dot(table, hot)
        part_ref[k, 0:64] = picked[0:64] + picked[128:192] + (own[128:192] + gate_w * cos[k : k + 1])
        part_ref[k, 64:128] = picked[64:128] + picked[192:256]


def prep_stage(odd, count, *held):
    return pl.pallas_call(
        prep_kernel,
        out_shape=(
            stay((256, CAP), BF16),
            stay((128, CAP), F32),
            stay((EXT, ARITY * CAP), BF16),
            stay((ARITY, 128, CAP), F32),
            stay((8, CAP), F32),
            stay((64, CAP), F32),
            stay((16, CAP), F32),
        ),
        in_specs=[SMEM, SMEM] + [VMEM] * 6,
        out_specs=(VMEM,) * 7,
        compiler_params=pltpu.CompilerParams(vmem_limit_bytes=24 << 20),
        name="prep_stage",
    )(odd, count, *(in_vmem(x) for x in held))


def angle_kernel(
    ga_ref, gb_ref, w_ref, own_ref, hot_ref, part_ref, live_ref, cot_live_ref, cos_ref,
    whole_ref, full_ref, edge_ref, dgw_ref,
    pick_ref, sig_ref, bonds_ref, slope_ref,
):
    w_t = w_ref[...]
    gh_t = jnp.concatenate([ga_ref[...], gb_ref[...]], axis=0).T
    high, low = two_parts(dot(w_t[:128], gh_t))
    table = jnp.concatenate([high, low], axis=1)
    for k in range(ARITY):
        far = hot_ref[CAP:, k * CAP : (k + 1) * CAP]
        pick_ref[k] = dot(table, jnp.concatenate([far, far], axis=0)) + part_ref[k]

    for at in (slice(0, 128), slice(128, 256)):
        live = live_ref[0:1, at]
        num = jnp.zeros((64, 128), F32)
        den = jnp.zeros((64, 128), F32)
        for k in range(ARITY):
            sig = sigmoid(pick_ref[k, 0:64, at])
            gate = sig * live
            num += gate * pick_ref[k, 64:128, at]
            den += gate
            sig_ref[k, :, at] = sig
        den = den + EPS
        agg = num / den
        z = own_ref[64:128, at] + agg
        s = sigmoid(z)
        dz = cot_live_ref[:, at] * (s * (1.0 + z * (1.0 - s)))
        dnum = dz / den
        dden = -(dnum * agg)
        bonds_ref[64:128, at] = dz.astype(BF16)
        slope_ref[0:64, at] = dnum
        slope_ref[64:128, at] = dden
    zero = jnp.zeros((64, 128), F32)
    dq2, dgw = [zero, zero], [zero, zero]
    acc = jnp.zeros((EXT, 128), F32)
    for first in range(0, ARITY, CHUNK):
        chunk = []
        for k in range(first, first + CHUNK):
            dpre, dmsg = [], []
            for n in (0, 1):
                at = slice(n * 128, (n + 1) * 128)
                dnum = slope_ref[0:64, at]
                sig = sig_ref[k, :, at]
                gate = sig * live_ref[0:1, at]
                dgate = dnum * pick_ref[k, 64:128, at] + slope_ref[64:128, at]
                change = dgate * gate * (1.0 - sig)
                dq2[n] += change
                dgw[n] += change * cos_ref[k : k + 1, at]
                dpre.append(change.astype(BF16))
                dmsg.append((gate * dnum).astype(BF16))
            chunk.append(jnp.concatenate([jnp.concatenate(dpre, axis=1), jnp.concatenate(dmsg, axis=1)], axis=0))
        acc += dot(hot_ref[:, first * CAP : (first + CHUNK) * CAP], jnp.concatenate(chunk, axis=1), 1, 1)
    dgw_ref[...] = jnp.concatenate(dgw, axis=1)
    bonds_ref[0:64] = jnp.concatenate(dq2, axis=1).astype(BF16)
    edge = acc.astype(BF16)
    full = jnp.concatenate([edge[:CAP], bonds_ref[...].T], axis=1)
    edge_far = edge[CAP:]
    full_ref[...] = full
    edge_ref[...] = edge_far
    whole_ref[:, :CAP] = dot(full, w_t).astype(BF16).T
    whole_ref[:, CAP:] = dot(edge_far, w_t[:128]).astype(BF16).T


def angle_stage(ga, gb, *prepared):
    return pl.pallas_call(
        angle_kernel,
        out_shape=(
            stay((256, EXT), BF16),
            stay((CAP, 256), BF16),
            stay((2 * GHOST, 128), BF16),
            stay((64, CAP), F32),
        ),
        in_specs=[VMEM] * 9,
        out_specs=(VMEM,) * 4,
        scratch_shapes=[
            pltpu.VMEM((ARITY, 128, CAP), F32),
            pltpu.VMEM((ARITY, 64, CAP), F32),
            pltpu.VMEM((128, CAP), BF16),
            pltpu.VMEM((128, CAP), F32),
        ],
        compiler_params=pltpu.CompilerParams(vmem_limit_bytes=24 << 20),
        name="angle_stage",
    )(in_vmem(ga), in_vmem(gb), *(in_vmem(x) for x in prepared))


def grads_kernel(odd_ref, ga_ref, gb_ref, h_t_ref, full_ref, edge_ref, dgw_ref, send_ref, keep_ref):
    odd = odd_ref[0]
    rows = 256 // NDOM
    m = lax.broadcasted_iota(jnp.int32, (256, 1), 0)
    i = lax.broadcasted_iota(jnp.int32, (256, 256), 1)
    half = jnp.where(m < 128, 1 - odd, odd)
    m = m & 127
    want = (m // rows) * (2 * rows) + rows * half + m % rows
    perm = (i == want).astype(F32).astype(BF16)
    full = full_ref[...]
    gh_t = jnp.concatenate([ga_ref[...], gb_ref[...]], axis=0).T
    own = dot(h_t_ref[...], full)
    own = jnp.concatenate([own[:, :128] + dot(gh_t, edge_ref[...]), own[:, 128:]], axis=1)
    high, low = two_parts(own)
    send_ref[0:128] = dot(perm[:128], high).astype(BF16)
    keep_ref[0:128] = dot(perm[128:], high) + dot(perm[128:], low)
    ones = jnp.ones((8, CAP), BF16)
    dgw_high, dgw_low = two_parts(dgw_ref[...])
    gate = dot(ones, dgw_high, 1, 1) + dot(ones, dgw_low, 1, 1)
    keep_ref[128:136] = jnp.concatenate([gate, jnp.zeros((8, 192), F32)], axis=1)
    gate_high, gate_low = two_parts(gate)
    row = jnp.concatenate([gate_high, gate_low, jnp.zeros((8, 128), BF16)], axis=1)
    send_ref[128:144] = jnp.concatenate([row, row], axis=0)


def grads_stage(odd, ga, gb, *found):
    return pl.pallas_call(
        grads_kernel,
        out_shape=(stay((144, 256), BF16), stay((136, 256), F32)),
        in_specs=[SMEM] + [VMEM] * 6,
        out_specs=(VMEM, VMEM),
        compiler_params=pltpu.CompilerParams(vmem_limit_bytes=24 << 20),
        name="grads_stage",
    )(odd, in_vmem(ga), in_vmem(gb), *found)


def pair_kernel(keep_ref, recv_ref, out_ref):
    out_ref[:, :256] = (keep_ref[0:128] + recv_ref[0:128].astype(F32)).astype(BF16)
    row = recv_ref[128:144].astype(F32)[0:8]
    gate = keep_ref[128:136][:, 0:64] + row[:, 0:64] + row[:, 64:128]
    high, low = two_parts(gate)
    out_ref[:, 256:] = jnp.broadcast_to(jnp.concatenate([high, low], axis=1)[0:1], (128, 128))


def pair_stage(keep, recv):
    return pl.pallas_call(
        pair_kernel,
        out_shape=jax.ShapeDtypeStruct((128, 384), BF16),
        in_specs=[VMEM, VMEM],
        out_specs=VMEM,
        compiler_params=pltpu.CompilerParams(vmem_limit_bytes=24 << 20),
        name="pair_stage",
    )(keep, in_vmem(recv))


def last_kernel(slots_ref, source_ref, target_ref, message_ref, self_ref, gate_ref):
    total = jnp.sum(slots_ref[...].astype(F32), axis=0)
    source_ref[...] = total[:, 0:64]
    message_ref[...] = total[:, 64:128]
    target_ref[...] = total[:, 128:192]
    self_ref[...] = total[:, 192:256]
    gate_ref[...] = total[0:1, 256:320] + total[0:1, 320:384]


def last_stage(slots):
    rows = slots.shape[1]
    square = jax.ShapeDtypeStruct((rows, 64), F32)
    return pl.pallas_call(
        last_kernel,
        out_shape=(square, square, square, square, jax.ShapeDtypeStruct((1, 64), F32)),
        in_specs=[VMEM],
        out_specs=(VMEM,) * 5,
        compiler_params=pltpu.CompilerParams(vmem_limit_bytes=24 << 20),
        name="last_stage",
    )(in_vmem(slots))


def swap_core(x):
    return lax.ppermute(x, DOM, [(i, i ^ 1) for i in range(NDOM)])


def swap_chip(x):
    return lax.ppermute(x, DOM, [(i, (i + 1) % NDOM if i % 2 else (i - 1) % NDOM) for i in range(NDOM)])


def per_device(
    bond_feats,
    cotangent,
    bond_count,
    source,
    cosine,
    w_source,
    w_target,
    w_message,
    w_self,
    gate_angle,
):
    odd = lax.axis_index("dom_2").astype(jnp.int32)
    is_odd = odd == 1
    odd = odd.reshape(1)
    to_a, to_b, src, cos, own_h, w_t, *rest = front_stage(
        odd,
        source.reshape(24, 128),
        cosine.reshape(24, 128),
        bond_feats,
        w_source.T,
        w_message.T,
        w_target.T,
        w_self.T,
        gate_angle[None, :],
        cotangent.T,
    )
    ghost_b = swap_chip(to_b)
    ghost_a = swap_core(to_a)
    h_t, *prepared = prep_stage(odd, bond_count, src, cos, own_h, w_t, *rest)
    prepared.insert(0, w_t)
    whole, *found = angle_stage(ghost_a, ghost_b, *prepared)
    tiles = lax.all_to_all(whole.reshape(4, 64, EXT), "wa", 0, 0, tiled=True)
    send, keep = grads_stage(odd, ghost_a, ghost_b, h_t, *found)
    recv = swap_core(send)
    slots = pair_stage(keep, recv).reshape(NDOM // 2, 256 // NDOM, 384)
    slots = lax.all_to_all(slots, CHIP, 0, 0, tiled=True)
    summed = tiles.astype(F32).sum(axis=0)
    to_a, to_b = summed[:, CAP : CAP + GHOST], summed[:, CAP + GHOST :]
    back_b = swap_chip(to_b)
    back_a = swap_core(to_a)
    g_source, g_target, g_message, g_self, g_gate = last_stage(slots)

    total = summed[:, :CAP] + prepared[-2]
    to_first = jnp.where(is_odd, back_a, back_b)
    to_last = jnp.where(is_odd, back_b, back_a)
    added = jnp.concatenate([to_first, jnp.zeros((64, CAP - 2 * GHOST), F32), to_last], axis=1)
    bond_grad = (total + added).astype(BF16).T
    return (bond_grad, g_source, g_target, g_message, g_self, g_gate[0])


def solution(mesh):
    finer = Mesh(mesh.devices.reshape(8, 8, 2, mesh.shape["wa"]), ("dom_0", "dom_1", "dom_2", "wa"))
    return jax.shard_map(
        per_device,
        mesh=finer,
        in_specs=(
            P(DOM, None),
            P(DOM, "wa"),
            P(DOM),
            P(DOM),
            P(DOM),
            P(None, "wa"),
            P(None, "wa"),
            P(None, "wa"),
            P(None, "wa"),
            P("wa"),
        ),
        out_specs=(P(DOM, "wa"), P(DOM, "wa"), P(DOM, "wa"), P(DOM, "wa"), P(DOM, "wa"), P("wa")),
        check_vma=False,
    )
```

```python
import jax
import jax.numpy as jnp
from jax import lax
from jax.experimental import pallas as pl
from jax.experimental.pallas import tpu as pltpu
from jax.sharding import Mesh
from jax.sharding import PartitionSpec as P


ARITY = 12
CHUNK = 12
GHOST = 32
CAP = 256
EXT = CAP + 2 * GHOST
DOM = ("dom_0", "dom_1", "dom_2")
CHIP = ("dom_0", "dom_1")
NDOM = 128
EPS = 1e-06
F32 = jnp.float32
BF16 = jnp.bfloat16
VMEM = pl.BlockSpec(memory_space=pltpu.VMEM)
SMEM = pl.BlockSpec(memory_space=pltpu.SMEM)
HBM = pl.BlockSpec(memory_space=pltpu.HBM)


def dot(a, b, ca=1, cb=0):
    return lax.dot_general(a, b, (((ca,), (cb,)), ((), ())), preferred_element_type=F32)


def sigmoid(v):
    return 1.0 / (1.0 + jnp.exp(-v))


def two_parts(v):
    high = v.astype(BF16)
    return high, (v - high.astype(F32)).astype(BF16)


def in_vmem(x):
    return pltpu.with_memory_space_constraint(x, pltpu.VMEM)


def in_hbm(x):
    return pltpu.with_memory_space_constraint(x, pltpu.HBM)


def stay(shape, dtype):
    return pltpu.VMEM(shape, dtype)


def live_row(count):
    bond = lax.broadcasted_iota(jnp.int32, (1, CAP), 1)
    return ((bond < count - GHOST) | (bond >= CAP - GHOST)).astype(F32)


def front_kernel(
    odd_ref, src_hbm, cos_hbm, h_hbm, ws_hbm, wm_hbm, wt_hbm, wf_hbm, gate_w_hbm, cot_hbm,
    to_a_ref, to_b_ref, src_t_ref, cos_t_ref, h_ref, w_ref, gate_w_ref, cot_ref,
    src_ref, cos_ref, sems,
):
    odd = odd_ref[0]
    at_a = pl.multiple_of((1 - odd) * (CAP - GHOST), GHOST)
    at_b = pl.multiple_of(odd * (CAP - GHOST), GHOST)
    pairs = [
        (src_hbm, src_ref),
        (cos_hbm, cos_ref),
        (h_hbm.at[pl.ds(at_b, GHOST)], to_b_ref),
        (h_hbm.at[pl.ds(at_a, GHOST)], to_a_ref),
        (h_hbm, h_ref),
        (gate_w_hbm, gate_w_ref),
        (cot_hbm, cot_ref),
    ]
    for n, ref in enumerate((ws_hbm, wm_hbm, wt_hbm, wf_hbm)):
        pairs.append((ref, w_ref.at[pl.ds(64 * n, 64)]))
    copies = [pltpu.make_async_copy(a, b, sems.at[n]) for n, (a, b) in enumerate(pairs)]
    for copy in copies:
        copy.start()
    for copy in copies[:2]:
        copy.wait()
    src_t_ref[...], cos_t_ref[...] = by_slot(src_ref, cos_ref)
    for copy in copies[2:]:
        copy.wait()


def front_stage(odd, *held):
    return pl.pallas_call(
        front_kernel,
        out_shape=(
            stay((GHOST, 256), BF16),
            stay((GHOST, 256), BF16),
            stay((16, CAP), jnp.int32),
            stay((16, CAP), F32),
            stay((CAP, 256), BF16),
            stay((256, 256), BF16),
            stay((1, 64), F32),
            stay((64, CAP), BF16),
        ),
        in_specs=[SMEM] + [HBM] * 9,
        out_specs=(VMEM,) * 8,
        scratch_shapes=[
            pltpu.VMEM((24, 128), jnp.int32),
            pltpu.VMEM((24, 128), F32),
            pltpu.SemaphoreType.DMA((11,)),
        ],
        compiler_params=pltpu.CompilerParams(vmem_limit_bytes=24 << 20),
        name="front_stage",
    )(odd, *(in_hbm(x) for x in held))


def by_slot(src_ref, cos_ref):
    def grouped(ref):
        return jnp.concatenate([ref[pl.ds(t, 8, stride=3), :] for t in range(3)], axis=1)

    cos = grouped(cos_ref)
    one, two = two_parts(cos)
    middle = EXT // 2
    src = (grouped(src_ref) - middle).astype(F32)
    parts = jnp.concatenate([src, one.astype(F32), two.astype(F32), jnp.zeros((8, 384), F32)], axis=0).astype(BF16)
    spot = lax.broadcasted_iota(jnp.int32, (384, CAP), 0)
    start = (lax.broadcasted_iota(jnp.int32, (1, CAP), 1) & 31) * ARITY
    inside = (spot >= start) & (spot < start + ARITY)
    slot = lax.broadcasted_iota(jnp.int32, (16, 384), 1) % ARITY
    slot = (slot == lax.broadcasted_iota(jnp.int32, (16, 384), 0)).astype(F32).astype(BF16)
    group = lax.broadcasted_iota(jnp.int32, (32, CAP), 0)
    wanted = lax.broadcasted_iota(jnp.int32, (32, CAP), 1) >> 5
    rows = []
    for n in range(3):
        pick = (group == wanted + 8 * n).astype(F32).astype(BF16)
        spread = jnp.where(inside, dot(parts, pick, 0, 0), 0.0).astype(BF16)
        rows.append(dot(slot, spread))
    return rows[0].astype(jnp.int32) + middle, rows[1] + rows[2]


def prep_kernel(
    odd_ref, count_ref, src_ref, cos_ref, h_ref, w_ref, gate_w_ref, cot_ref,
    h_t_ref, own_ref, hot_ref, part_ref, live_ref, cot_live_ref,
):
    odd = odd_ref[0]
    src, cos = src_ref[...], cos_ref[...]
    low_base = jnp.where(odd == 1, CAP, CAP + GHOST)
    high_base = jnp.where(odd == 1, CAP + GHOST, CAP)
    row = jnp.where(
        src < GHOST,
        src + low_base,
        jnp.where(src >= CAP + GHOST, src - (CAP + GHOST) + high_base, src - GHOST),
    )
    near_row = row.astype(F32).astype(BF16)
    far_row = (row - CAP).astype(F32).astype(BF16)
    near_id = lax.broadcasted_iota(jnp.int32, (CAP, CAP), 0).astype(F32).astype(BF16)
    far_id = lax.broadcasted_iota(jnp.int32, (2 * GHOST, CAP), 0).astype(F32).astype(BF16)
    one, zero = jnp.ones((), BF16), jnp.zeros((), BF16)
    live = live_row(count_ref[0])
    live_ref[...] = jnp.broadcast_to(live, (8, CAP))
    cot_live_ref[...] = cot_ref[...].astype(F32) * live
    h_t = h_ref[...].T
    w_t = w_ref[...]
    h_t_ref[...] = h_t
    own = dot(w_t, h_t)
    own_ref[...] = own[128:]
    high, low = two_parts(own[:128])
    table = jnp.concatenate([high, low], axis=0)
    eye = lax.broadcasted_iota(jnp.int32, (64, 64), 0) == lax.broadcasted_iota(jnp.int32, (64, 64), 1)
    gate_w = jnp.sum(jnp.where(eye, gate_w_ref[...], 0.0), axis=1, keepdims=True)
    for k in range(ARITY):
        at = slice(k * CAP, (k + 1) * CAP)
        hot = jnp.where(near_id == near_row[k : k + 1], one, zero)
        hot_ref[:CAP, at] = hot
        hot_ref[CAP:, at] = jnp.where(far_id == far_row[k : k + 1], one, zero)
        picked = dot(table, hot)
        part_ref[k, 0:64] = picked[0:64] + picked[128:192] + (own[128:192] + gate_w * cos[k : k + 1])
        part_ref[k, 64:128] = picked[64:128] + picked[192:256]


def prep_stage(odd, count, *held):
    return pl.pallas_call(
        prep_kernel,
        out_shape=(
            stay((256, CAP), BF16),
            stay((128, CAP), F32),
            stay((EXT, ARITY * CAP), BF16),
            stay((ARITY, 128, CAP), F32),
            stay((8, CAP), F32),
            stay((64, CAP), F32),
        ),
        in_specs=[SMEM, SMEM] + [VMEM] * 6,
        out_specs=(VMEM,) * 6,
        compiler_params=pltpu.CompilerParams(vmem_limit_bytes=24 << 20),
        name="prep_stage",
    )(odd, count, *(in_vmem(x) for x in held))


def angle_kernel(
    ga_ref, gb_ref, w_ref, own_ref, hot_ref, part_ref, live_ref, cot_live_ref, cos_ref,
    whole_ref, full_ref, edge_ref, dgw_ref,
    pick_ref, sig_ref, bonds_ref, slope_ref,
):
    w_t = w_ref[...]
    gh_t = jnp.concatenate([ga_ref[...], gb_ref[...]], axis=0).T
    high, low = two_parts(dot(w_t[:128], gh_t))
    table = jnp.concatenate([high, low], axis=1)
    for k in range(ARITY):
        far = hot_ref[CAP:, k * CAP : (k + 1) * CAP]
        pick_ref[k] = dot(table, jnp.concatenate([far, far], axis=0)) + part_ref[k]

    for at in (slice(0, 128), slice(128, 256)):
        live = live_ref[0:1, at]
        num = jnp.zeros((64, 128), F32)
        den = jnp.zeros((64, 128), F32)
        for k in range(ARITY):
            sig = sigmoid(pick_ref[k, 0:64, at])
            gate = sig * live
            num += gate * pick_ref[k, 64:128, at]
            den += gate
            sig_ref[k, :, at] = sig
        den = den + EPS
        agg = num / den
        z = own_ref[64:128, at] + agg
        s = sigmoid(z)
        dz = cot_live_ref[:, at] * (s * (1.0 + z * (1.0 - s)))
        dnum = dz / den
        dden = -(dnum * agg)
        bonds_ref[64:128, at] = dz.astype(BF16)
        slope_ref[0:64, at] = dnum
        slope_ref[64:128, at] = dden
    zero = jnp.zeros((64, 128), F32)
    dq2, dgw = [zero, zero], [zero, zero]
    acc = jnp.zeros((EXT, 128), F32)
    for first in range(0, ARITY, CHUNK):
        chunk = []
        for k in range(first, first + CHUNK):
            dpre, dmsg = [], []
            for n in (0, 1):
                at = slice(n * 128, (n + 1) * 128)
                dnum = slope_ref[0:64, at]
                sig = sig_ref[k, :, at]
                gate = sig * live_ref[0:1, at]
                dgate = dnum * pick_ref[k, 64:128, at] + slope_ref[64:128, at]
                change = dgate * gate * (1.0 - sig)
                dq2[n] += change
                dgw[n] += change * cos_ref[k : k + 1, at]
                dpre.append(change.astype(BF16))
                dmsg.append((gate * dnum).astype(BF16))
            chunk.append(jnp.concatenate([jnp.concatenate(dpre, axis=1), jnp.concatenate(dmsg, axis=1)], axis=0))
        acc += dot(hot_ref[:, first * CAP : (first + CHUNK) * CAP], jnp.concatenate(chunk, axis=1), 1, 1)
    dgw_ref[...] = jnp.concatenate(dgw, axis=1)
    bonds_ref[0:64] = jnp.concatenate(dq2, axis=1).astype(BF16)
    edge = acc.astype(BF16)
    full = jnp.concatenate([edge[:CAP], bonds_ref[...].T], axis=1)
    edge_far = edge[CAP:]
    full_ref[...] = full
    edge_ref[...] = edge_far
    whole_ref[:, :CAP] = dot(full, w_t).astype(BF16).T
    whole_ref[:, CAP:] = dot(edge_far, w_t[:128]).astype(BF16).T


def angle_stage(ga, gb, *prepared):
    return pl.pallas_call(
        angle_kernel,
        out_shape=(
            stay((256, EXT), BF16),
            stay((CAP, 256), BF16),
            stay((2 * GHOST, 128), BF16),
            stay((64, CAP), F32),
        ),
        in_specs=[VMEM] * 9,
        out_specs=(VMEM,) * 4,
        scratch_shapes=[
            pltpu.VMEM((ARITY, 128, CAP), F32),
            pltpu.VMEM((ARITY, 64, CAP), F32),
            pltpu.VMEM((128, CAP), BF16),
            pltpu.VMEM((128, CAP), F32),
        ],
        compiler_params=pltpu.CompilerParams(vmem_limit_bytes=24 << 20),
        name="angle_stage",
    )(in_vmem(ga), in_vmem(gb), *(in_vmem(x) for x in prepared))


def grads_kernel(odd_ref, ga_ref, gb_ref, h_t_ref, full_ref, edge_ref, dgw_ref, send_ref, keep_ref):
    odd = odd_ref[0]
    rows = 256 // NDOM
    m = lax.broadcasted_iota(jnp.int32, (256, 1), 0)
    i = lax.broadcasted_iota(jnp.int32, (256, 256), 1)
    half = jnp.where(m < 128, 1 - odd, odd)
    m = m & 127
    want = (m // rows) * (2 * rows) + rows * half + m % rows
    perm = (i == want).astype(F32).astype(BF16)
    full = full_ref[...]
    gh_t = jnp.concatenate([ga_ref[...], gb_ref[...]], axis=0).T
    own = dot(h_t_ref[...], full)
    own = jnp.concatenate([own[:, :128] + dot(gh_t, edge_ref[...]), own[:, 128:]], axis=1)
    high, low = two_parts(own)
    send_ref[0:128] = dot(perm[:128], high).astype(BF16)
    keep_ref[0:128] = dot(perm[128:], high) + dot(perm[128:], low)
    ones = jnp.ones((8, CAP), BF16)
    dgw_high, dgw_low = two_parts(dgw_ref[...])
    gate = dot(ones, dgw_high, 1, 1) + dot(ones, dgw_low, 1, 1)
    keep_ref[128:136] = jnp.concatenate([gate, jnp.zeros((8, 192), F32)], axis=1)
    gate_high, gate_low = two_parts(gate)
    row = jnp.concatenate([gate_high, gate_low, jnp.zeros((8, 128), BF16)], axis=1)
    send_ref[128:144] = jnp.concatenate([row, row], axis=0)


def grads_stage(odd, ga, gb, *found):
    return pl.pallas_call(
        grads_kernel,
        out_shape=(stay((144, 256), BF16), stay((136, 256), F32)),
        in_specs=[SMEM] + [VMEM] * 6,
        out_specs=(VMEM, VMEM),
        compiler_params=pltpu.CompilerParams(vmem_limit_bytes=24 << 20),
        name="grads_stage",
    )(odd, in_vmem(ga), in_vmem(gb), *found)


def pair_kernel(keep_ref, recv_ref, out_ref):
    out_ref[:, :256] = (keep_ref[0:128] + recv_ref[0:128].astype(F32)).astype(BF16)
    row = recv_ref[128:144].astype(F32)[0:8]
    gate = keep_ref[128:136][:, 0:64] + row[:, 0:64] + row[:, 64:128]
    high, low = two_parts(gate)
    out_ref[:, 256:] = jnp.broadcast_to(jnp.concatenate([high, low], axis=1)[0:1], (128, 128))


def pair_stage(keep, recv):
    return pl.pallas_call(
        pair_kernel,
        out_shape=jax.ShapeDtypeStruct((128, 384), BF16),
        in_specs=[VMEM, VMEM],
        out_specs=VMEM,
        compiler_params=pltpu.CompilerParams(vmem_limit_bytes=24 << 20),
        name="pair_stage",
    )(keep, in_vmem(recv))


def last_kernel(slots_ref, source_ref, target_ref, message_ref, self_ref, gate_ref):
    total = jnp.sum(slots_ref[...].astype(F32), axis=0)
    source_ref[...] = total[:, 0:64]
    message_ref[...] = total[:, 64:128]
    target_ref[...] = total[:, 128:192]
    self_ref[...] = total[:, 192:256]
    gate_ref[...] = total[0:1, 256:320] + total[0:1, 320:384]


def last_stage(slots):
    rows = slots.shape[1]
    square = jax.ShapeDtypeStruct((rows, 64), F32)
    return pl.pallas_call(
        last_kernel,
        out_shape=(square, square, square, square, jax.ShapeDtypeStruct((1, 64), F32)),
        in_specs=[VMEM],
        out_specs=(VMEM,) * 5,
        compiler_params=pltpu.CompilerParams(vmem_limit_bytes=24 << 20),
        name="last_stage",
    )(in_vmem(slots))


def swap_core(x):
    return lax.ppermute(x, DOM, [(i, i ^ 1) for i in range(NDOM)])


def swap_chip(x):
    return lax.ppermute(x, DOM, [(i, (i + 1) % NDOM if i % 2 else (i - 1) % NDOM) for i in range(NDOM)])


def per_device(
    bond_feats,
    cotangent,
    bond_count,
    source,
    cosine,
    w_source,
    w_target,
    w_message,
    w_self,
    gate_angle,
):
    odd = lax.axis_index("dom_2").astype(jnp.int32)
    is_odd = odd == 1
    odd = odd.reshape(1)
    to_a, to_b, src, cos, own_h, w_t, *rest = front_stage(
        odd,
        source.reshape(24, 128),
        cosine.reshape(24, 128),
        bond_feats,
        w_source.T,
        w_message.T,
        w_target.T,
        w_self.T,
        gate_angle[None, :],
        cotangent.T,
    )
    ghost_b = swap_chip(to_b)
    ghost_a = swap_core(to_a)
    h_t, *prepared = prep_stage(odd, bond_count, src, cos, own_h, w_t, *rest)
    prepared = [w_t, *prepared, cos]
    whole, *found = angle_stage(ghost_a, ghost_b, *prepared)
    tiles = lax.all_to_all(whole.reshape(4, 64, EXT), "wa", 0, 0, tiled=True)
    send, keep = grads_stage(odd, ghost_a, ghost_b, h_t, *found)
    recv = swap_core(send)
    slots = pair_stage(keep, recv).reshape(NDOM // 2, 256 // NDOM, 384)
    slots = lax.all_to_all(slots, CHIP, 0, 0, tiled=True)
    summed = tiles.astype(F32).sum(axis=0)
    to_a, to_b = summed[:, CAP : CAP + GHOST], summed[:, CAP + GHOST :]
    back_b = swap_chip(to_b)
    back_a = swap_core(to_a)
    g_source, g_target, g_message, g_self, g_gate = last_stage(slots)

    total = summed[:, :CAP] + prepared[-2]
    to_first = jnp.where(is_odd, back_a, back_b)
    to_last = jnp.where(is_odd, back_b, back_a)
    added = jnp.concatenate([to_first, jnp.zeros((64, CAP - 2 * GHOST), F32), to_last], axis=1)
    bond_grad = (total + added).astype(BF16).T
    return (bond_grad, g_source, g_target, g_message, g_self, g_gate[0])


def solution(mesh):
    finer = Mesh(mesh.devices.reshape(8, 8, 2, mesh.shape["wa"]), ("dom_0", "dom_1", "dom_2", "wa"))
    return jax.shard_map(
        per_device,
        mesh=finer,
        in_specs=(
            P(DOM, None),
            P(DOM, "wa"),
            P(DOM),
            P(DOM),
            P(DOM),
            P(None, "wa"),
            P(None, "wa"),
            P(None, "wa"),
            P(None, "wa"),
            P("wa"),
        ),
        out_specs=(P(DOM, "wa"), P(DOM, "wa"), P(DOM, "wa"), P(DOM, "wa"), P(DOM, "wa"), P("wa")),
        check_vma=False,
    )
```
